256 devices in a mesh: row: 32 (over x, z), col: 8 (over y, core).
Axes of the slice: x: 4, y: 4, z: 8, core: 2. Of those that a mesh axis runs over, the one named last changes fastest.
Arguments:
- latent: bfloat16 [1024, 1024, 128], P('row', 'col'), may hold values from -140 to 140
- group_norm_gain: float32 [128], replicated, may hold values from 0.25 to 1.75
- group_norm_bias: float32 [128], replicated, may hold values from -2.5 to 2.5
- decoder_weight: bfloat16 [3, 3, 128, 3], replicated, may hold values from -0.1875 to 0.1875
- decoder_bias: float32 [3], replicated, may hold values from -2.5 to 2.5
- first_weight: bfloat16 [3, 3, 3, 64], replicated, may hold values from -1.25 to 1.25
- first_bias: float32 [64], replicated, may hold values from -2.5 to 2.5
- second_weight: bfloat16 [3, 3, 64, 64], replicated, may hold values from -0.25 to 0.25
- second_bias: float32 [64], replicated, may hold values from -2.5 to 2.5
- third_weight: bfloat16 [3, 3, 64, 128], replicated, may hold values from -0.25 to 0.25
- third_bias: float32 [128], replicated, may hold values from -2.5 to 2.5
- fourth_weight: bfloat16 [3, 3, 128, 128], replicated, may hold values from -0.1875 to 0.1875
- fourth_bias: float32 [128], replicated, may hold values from -2.5 to 2.5
- exemplar_low: float32 [64, 64], replicated, may hold values from -1.2 to 1.2
- exemplar_high: float32 [128, 128], replicated, may hold values from -1.2 to 1.2
Outputs:
- latent_grad: bfloat16 [1024, 1024, 128], P('row', 'col')
- style_loss: float32 [], replicated
The draws below stay inside these ranges and needn't reach their ends.
All inputs are finite; a program needn't handle non-finite values.
Results may differ from the reference program's by a relative error of at most 0.014.
Values may be sent and summed in bfloat16 or wider, within the bound.
No kernel may reach another device: no remote copies, remote signals or barrier semaphores. Data moves between devices by JAX's collectives and lax.ppermute only.
A program may use at most 64 MiB of HBM per device.

```python
import jax
import jax.numpy as jnp
from jax import lax

DECODER_CHANNELS = 128
C1 = 64
C2 = 128
GROUPS = 32
TR = 32
TC = 128
IMAGE_ROWS = 1024
IMAGE_COLUMNS = 1024


def draw_latent(key, part):
    key_base = jax.random.fold_in(key, 0)
    key_shift = jax.random.fold_in(key, 2)
    key_trow = jax.random.fold_in(key, 3)
    key_tcol = jax.random.fold_in(key, 4)
    along_rows = jnp.arange(IMAGE_ROWS, dtype=jnp.float32) / max(IMAGE_ROWS - 1, 1)
    along_cols = jnp.arange(IMAGE_COLUMNS, dtype=jnp.float32) / max(IMAGE_COLUMNS - 1, 1)
    ramp = jnp.exp(1.0986 * along_rows)[:, None, None] * jnp.exp(0.5 * along_cols)[None, :, None]
    shift = 1.5 * jax.random.uniform(key_shift, (1, 1, DECODER_CHANNELS), jnp.float32, -1.0, 1.0)
    heavy_row = jax.random.randint(key_trow, (), 0, IMAGE_ROWS // TR)
    heavy_col = jax.random.randint(key_tcol, (), 0, IMAGE_COLUMNS // TC)
    row_index = jnp.arange(IMAGE_ROWS, dtype=jnp.int32) // TR
    col_index = jnp.arange(IMAGE_COLUMNS, dtype=jnp.int32) // TC
    heavy_mask = (row_index == heavy_row).astype(jnp.float32)[:, None, None] * (col_index == heavy_col).astype(jnp.float32)[None, :, None]
    boost = 1.0 + 3.0 * heavy_mask
    base = jnp.clip(jax.random.normal(key_base, (IMAGE_ROWS, IMAGE_COLUMNS, DECODER_CHANNELS), jnp.float32), -4.0, 4.0)
    return (base * ramp * boost + shift).astype(jnp.bfloat16)


def gaussian(own_key, extent, scale, reach, kind=jnp.bfloat16):
    return jnp.clip(scale * jax.random.normal(own_key, extent, jnp.float32), -reach, reach).astype(kind)


def setup_inputs(seed: int = 0) -> dict:
    keys = jax.random.split(jax.random.key(seed), 16)
    return {
        "latent": draw_latent(jax.random.fold_in(keys[15], 71), 0),
        "group_norm_gain": jnp.clip(1.0 + 0.15 * jax.random.normal(keys[1], (DECODER_CHANNELS,), jnp.float32), 0.25, 1.75),
        "group_norm_bias": gaussian(keys[2], (DECODER_CHANNELS,), 0.5, 2.5, jnp.float32),
        "decoder_weight": gaussian(keys[3], (3, 3, DECODER_CHANNELS, 3), (9 * DECODER_CHANNELS) ** -0.5, 0.1875),
        "decoder_bias": gaussian(keys[4], (3,), 0.3, 2.5, jnp.float32),
        "first_weight": gaussian(keys[5], (3, 3, 3, C1), 27 ** -0.5, 1.25),
        "first_bias": gaussian(keys[6], (C1,), 0.3, 2.5, jnp.float32),
        "second_weight": gaussian(keys[7], (3, 3, C1, C1), (9 * C1) ** -0.5, 0.25),
        "second_bias": gaussian(keys[8], (C1,), 0.3, 2.5, jnp.float32),
        "third_weight": gaussian(keys[9], (3, 3, C1, C2), (9 * C1) ** -0.5, 0.25),
        "third_bias": gaussian(keys[10], (C2,), 0.3, 2.5, jnp.float32),
        "fourth_weight": gaussian(keys[11], (3, 3, C2, C2), (9 * C2) ** -0.5, 0.1875),
        "fourth_bias": gaussian(keys[12], (C2,), 0.3, 2.5, jnp.float32),
        "exemplar_low": gaussian(keys[13], (C1, C1), 0.2, 1.2, jnp.float32),
        "exemplar_high": gaussian(keys[14], (C2, C2), 0.2, 1.2, jnp.float32),
    }


eps_norm = 1e-05
pix_mean = (0.485, 0.456, 0.406)
pix_std = (0.229, 0.224, 0.225)

def gelu_value(pre):
    return pre * 0.5 * (1.0 + lax.erf(pre * 0.7071067811865476))

def gelu_slope(pre):
    return 0.5 * (1.0 + lax.erf(pre * 0.7071067811865476)) + pre * jnp.exp(-0.5 * pre * pre) * 0.3989422804014327

def silu_slope(value):
    sig = jax.nn.sigmoid(value)
    return sig * (1.0 + value * (1.0 - sig))

def conv_same(source, kernel):
    padded = jnp.pad(source.astype(jnp.float32), ((1, 1), (1, 1), (0, 0)))
    return lax.conv_general_dilated(padded[None], kernel.astype(jnp.float32), (1, 1), 'VALID', dimension_numbers=('NHWC', 'HWIO', 'NHWC'), precision=lax.Precision.HIGHEST)[0]

def conv_back(source, kernel):
    return conv_same(source, jnp.transpose(kernel[::-1, ::-1], (0, 1, 3, 2)))

def gram_of(feature):
    flat = feature.reshape(-1, feature.shape[-1]).astype(jnp.float32)
    return jnp.dot(flat.T, flat, precision=lax.Precision.HIGHEST)

def reference(latent, group_norm_gain, group_norm_bias, decoder_weight, decoder_bias, first_weight, first_bias, second_weight, second_bias, third_weight, third_bias, fourth_weight, fourth_bias, exemplar_low, exemplar_high):
    group_view = latent.astype(jnp.float32).reshape(IMAGE_ROWS * IMAGE_COLUMNS, GROUPS, DECODER_CHANNELS // GROUPS)
    element_count = IMAGE_ROWS * IMAGE_COLUMNS * (DECODER_CHANNELS // GROUPS)
    group_mean = lax.optimization_barrier(jnp.sum(group_view, axis=(0, 2))) / element_count
    msq_g = lax.optimization_barrier(jnp.sum(group_view * group_view, axis=(0, 2))) / element_count
    inverse_deviation = 1.0 / jnp.sqrt(msq_g - group_mean * group_mean + eps_norm)
    normed_input = (group_view - group_mean[None, :, None]) * inverse_deviation[None, :, None]
    normed_input_whole = normed_input.reshape(IMAGE_ROWS, IMAGE_COLUMNS, DECODER_CHANNELS)
    before_norm_input = group_norm_gain * normed_input_whole + group_norm_bias
    activated = jax.nn.silu(before_norm_input).astype(jnp.bfloat16)
    rgb = conv_same(activated, decoder_weight) + decoder_bias
    color_mean = jnp.array(pix_mean, jnp.float32)
    color_std = jnp.array(pix_std, jnp.float32)
    pixels = (((rgb + 1.0) * 0.5 - color_mean) / color_std).astype(jnp.bfloat16)
    pre_one = conv_same(pixels, first_weight) + first_bias
    feat_one = gelu_value(pre_one).astype(jnp.bfloat16)
    pre_two = conv_same(feat_one, second_weight) + second_bias
    feat_two = gelu_value(pre_two).astype(jnp.bfloat16)
    gram_low = gram_of(feat_two) / (IMAGE_ROWS * IMAGE_COLUMNS)
    pooled = feat_two.astype(jnp.float32).reshape(IMAGE_ROWS // 2, 2, IMAGE_COLUMNS // 2, 2, C1).mean(axis=(1, 3)).astype(jnp.bfloat16)
    pre_three = conv_same(pooled, third_weight) + third_bias
    feat_three = gelu_value(pre_three).astype(jnp.bfloat16)
    pre_four = conv_same(feat_three, fourth_weight) + fourth_bias
    feat_four = gelu_value(pre_four).astype(jnp.bfloat16)
    gram_high = gram_of(feat_four) / (IMAGE_ROWS * IMAGE_COLUMNS // 4)
    gap_low = gram_low - exemplar_low
    gap_high = gram_high - exemplar_high
    sym_low = gap_low + gap_low.T
    sym_high = gap_high + gap_high.T
    style_loss = jnp.sum(gap_low * gap_low) / (C1 * C1) + jnp.sum(gap_high * gap_high) / (C2 * C2)
    grad_four = 2.0 * jnp.dot(feat_four.reshape(-1, C2).astype(jnp.float32), sym_high, precision=lax.Precision.HIGHEST).reshape(IMAGE_ROWS // 2, IMAGE_COLUMNS // 2, C2)
    back_four = (grad_four * gelu_slope(pre_four)).astype(jnp.bfloat16)
    back_three = (conv_back(back_four, fourth_weight) * gelu_slope(pre_three)).astype(jnp.bfloat16)
    grad_pool = conv_back(back_three, third_weight)
    spread = jnp.repeat(jnp.repeat(grad_pool, 2, axis=0), 2, axis=1) * 0.25
    gram_term = 2.0 * jnp.dot(feat_two.reshape(-1, C1).astype(jnp.float32), sym_low, precision=lax.Precision.HIGHEST).reshape(IMAGE_ROWS, IMAGE_COLUMNS, C1)
    back_two = ((spread + gram_term) * gelu_slope(pre_two)).astype(jnp.bfloat16)
    back_one = (conv_back(back_two, second_weight) * gelu_slope(pre_one)).astype(jnp.bfloat16)
    back_rgb = (conv_back(back_one, first_weight) * (0.5 / color_std)).astype(jnp.bfloat16)
    grad_act = conv_back(back_rgb, decoder_weight)
    dxhat = grad_act * silu_slope(before_norm_input) * group_norm_gain
    group_view_gradient = dxhat.reshape(IMAGE_ROWS * IMAGE_COLUMNS, GROUPS, DECODER_CHANNELS // GROUPS)
    mean_first_pass = lax.optimization_barrier(jnp.sum(group_view_gradient, axis=(0, 2))) / element_count
    mean_second_pass = lax.optimization_barrier(jnp.sum(group_view_gradient * normed_input, axis=(0, 2))) / element_count
    step_output = inverse_deviation[None, :, None] * (group_view_gradient - mean_first_pass[None, :, None] - normed_input * mean_second_pass[None, :, None])
    return (step_output.reshape(IMAGE_ROWS, IMAGE_COLUMNS, DECODER_CHANNELS).astype(jnp.bfloat16), style_loss)
```

```python
import jax
import jax.numpy as jnp
from jax import lax
from jax.experimental import pallas as pl
from jax.experimental.pallas import tpu as pltpu
from jax.sharding import PartitionSpec as P

GROUPS = 32
EPS = 1e-05
PIX_MEAN = (0.485, 0.456, 0.406)
PIX_STD = (0.229, 0.224, 0.225)
HALO = 16
F32 = jnp.float32
BF16 = jnp.bfloat16
INTERPRET = False
HIGH = lax.Precision.HIGHEST


def padded_dy(w, before, after):
    return jnp.pad(w, ((before, after), (0, 0), (0, 0), (0, 0)))


def flipped(w):
    return jnp.transpose(w[::-1, ::-1], (0, 1, 3, 2))


def pack_stream(w, order):
    wz = padded_dy(w, 1, 1)
    both = jnp.stack([wz[1:5], wz[0:4]], axis=0)
    both = jnp.stack([both[:, j] for j in order], axis=0)
    cin, cout = w.shape[2], w.shape[3]
    return jnp.transpose(both, (0, 3, 2, 1, 4)).reshape(4 * cin, 6 * cout)


def pack_narrow_out(w):
    cin, cout = w.shape[2], w.shape[3]
    wz = jnp.pad(w, ((2, 2), (0, 0), (0, 0), (0, 4 - cout)))
    parts = [wz[i - q - 2 * s + 3] for s in (0, -1, 1) for q in (0, 1) for i in (0, 1)]
    v = jnp.stack(parts, 0).reshape(3, 2, 2, 3, cin, 4)
    return jnp.transpose(v, (0, 3, 1, 5, 2, 4)).reshape(72, 2 * cin)


def pack_narrow_in(w):
    cin, cout = w.shape[2], w.shape[3]
    wz = jnp.pad(w, ((2, 2), (0, 0), (0, 4 - cin), (0, 0)))
    parts = [wz[2 * s + i - q + 3] for s in (-1, 0, 1) for i in (0, 1) for q in (0, 1)]
    v = jnp.stack(parts, 0).reshape(3, 2, 2, 3, 4, cout)
    v = jnp.transpose(v, (0, 3, 1, 4, 2, 5)).reshape(3, 24, 2 * cout)
    return jnp.pad(v, ((0, 0), (0, 8), (0, 0))).reshape(96, 2 * cout)


def iota(shape, axis):
    return lax.broadcasted_iota(jnp.int32, shape, axis)


def group_rows(s, q, channels):
    per = channels // GROUPS
    c = iota((channels, 128), 0) // per
    l = iota((channels, 128), 1)
    g1 = jnp.where(l == c, 1.0, 0.0).astype(F32)
    g2 = jnp.where(l == c + GROUPS, 1.0, 0.0).astype(F32)
    out = jnp.dot(s, g1, precision=HIGH, preferred_element_type=F32)
    out = out + jnp.dot(q, g2, precision=HIGH, preferred_element_type=F32)
    return jnp.sum(out, axis=0, keepdims=True)


def group_values(rows, channels, count):
    per = channels // GROUPS
    tot = jnp.sum(rows, axis=0, keepdims=True) * (1.0 / count)
    tot = jnp.broadcast_to(tot, (8, 128))
    l = iota((128, channels), 0)
    c = iota((128, channels), 1) // per
    e1 = jnp.where(l == c, 1.0, 0.0).astype(F32)
    e2 = jnp.where(l == c + GROUPS, 1.0, 0.0).astype(F32)
    a = jnp.dot(tot, e1, precision=HIGH, preferred_element_type=F32)[0:1]
    b = jnp.dot(tot, e2, precision=HIGH, preferred_element_type=F32)[0:1]
    return a, b


def norm_values(rows, channels, count):
    mean, msq = group_values(rows, channels, count)
    return mean, lax.rsqrt(msq - mean * mean + EPS)


def gelu_both(a):
    e = jnp.exp(a * a * -0.5)
    t = 1.0 / (1.0 + jnp.abs(a) * (0.3275911 * 0.7071067811865476))
    poly = t * (
        0.5 * 0.254829592
        + t
        * (0.5 * -0.284496736 + t * (0.5 * 1.421413741 + t * (0.5 * -1.453152027 + t * (0.5 * 1.061405429))))
    )
    q = poly * e
    phi = jnp.where(a >= 0.0, 1.0 - q, q)
    return a * phi, phi + a * e * 0.3989422804014327


def taps(p, n):
    m = p.shape[0]
    return pltpu.roll(p[:, 0:n], 1, 0) + p[:, n : 2 * n] + pltpu.roll(p[:, 2 * n : 3 * n], m - 1, 0)


def lane_taps(c):
    return pltpu.roll(c[0:8], 1, 1) + c[8:16] + pltpu.roll(c[16:24], 255, 1)


def nt(a, b):
    return lax.dot_general(a, b, (((1,), (1,)), ((), ())), preferred_element_type=F32)


def tn(a, b):
    return lax.dot_general(a, b, (((0,), (0,)), ((), ())), preferred_element_type=F32)


def loop(lo, hi, body):
    lax.fori_loop(lo, hi, lambda i, c: (body(i), c)[1], 0)


def color_column(values):
    c = iota((8, 1), 0) % 4
    out = jnp.zeros((8, 1), F32)
    for k, v in enumerate(values):
        out = jnp.where(c == k, v, out)
    return out


def stats_kernel(n, x_ref, o_ref):
    rows, cols, channels = x_ref.shape

    def body(r, carry):
        s, q = carry
        x = x_ref[r].astype(F32).reshape(cols // 8, 8, channels)
        return s + jnp.sum(x, axis=0), q + jnp.sum(x * x, axis=0)

    z = jnp.zeros((8, channels), F32)
    s, q = lax.fori_loop(0, rows, body, (z, z))
    o_ref[...] = jnp.broadcast_to(group_rows(s, q, channels), (n, 128))


def forward_kernel(
    dims,
    idx,
    dbias,
    lat_hbm,
    up,
    down,
    left,
    right,
    ul,
    ur,
    dl,
    dr,
    stats,
    vecs,
    wd,
    w1,
    w2,
    w3,
    w4,
    gram,
    slope1,
    feat2,
    slope2,
    slope3,
    feat4,
    slope4,
    sact,
    lat,
    tt,
    pixcol,
    y1,
    f2,
    yp,
    f3,
    fm,
    sems,
):
    rows, cols, image_rows, image_cols, count = dims
    h = HALO
    width = cols + 2 * h
    half = width // 2
    pairs = (rows + 2 * h) // 2
    pieces = (
        (lat_hbm, lat.at[pl.ds(h, rows), pl.ds(h, cols)]),
        (up, lat.at[pl.ds(0, h), pl.ds(h, cols)]),
        (down, lat.at[pl.ds(h + rows, h), pl.ds(h, cols)]),
        (left, lat.at[pl.ds(h, rows), pl.ds(0, h)]),
        (right, lat.at[pl.ds(h, rows), pl.ds(h + cols, h)]),
        (ul, lat.at[pl.ds(0, h), pl.ds(0, h)]),
        (ur, lat.at[pl.ds(0, h), pl.ds(h + cols, h)]),
        (dl, lat.at[pl.ds(h + rows, h), pl.ds(0, h)]),
        (dr, lat.at[pl.ds(h + rows, h), pl.ds(h + cols, h)]),
    )
    copies = [pltpu.make_async_copy(a, b, sems.at[i]) for i, (a, b) in enumerate(pieces)]
    for c in copies:
        c.start()

    tt[:, :, 128:256] = jnp.zeros((pairs, 72, 128), F32)
    pixcol[...] = jnp.zeros(pixcol.shape, BF16)
    yp[...] = jnp.zeros(yp.shape, BF16)

    row0 = idx[0] * rows - h
    col0 = idx[1] * cols - h

    def valid_rows(r):
        return jnp.where((row0 + r >= 0) & (row0 + r < image_rows), 1.0, 0.0).astype(F32)

    def col_mask(n, step, lanes):
        c = col0 + step * iota((n, lanes), 0)
        return jnp.where((c >= 0) & (c < image_cols), 1.0, 0.0).astype(F32)

    cmask = col_mask(width, 1, 128)
    hmask = col_mask(half, 2, 128)
    lane = iota((8, 256), 1)
    lmask = jnp.where((col0 + lane >= 0) & (col0 + lane < image_cols) & (lane < width), 1.0, 0.0)
    lmask = lmask.astype(F32)

    mean, rstd = norm_values(stats[...], 128, count)
    gain = vecs[0:1]
    scale = rstd * gain
    shift = vecs[1:2] - mean * scale
    b1, b2, b3, b4 = vecs[2:3], vecs[3:4], vecs[4:5], vecs[5:6]

    for c in copies:
        c.wait()

    def act_row(r):
        t = lat[r].astype(F32) * scale + shift
        sig = 0.5 * jnp.tanh(0.5 * t) + 0.5
        return t, sig

    def decode(p):
        parts = []
        m = cmask * valid_rows(2 * p)
        for i in range(2):
            t, sig = act_row(2 * p + i)
            parts.append((t * sig * m).astype(BF16))
        tt[p, :, 0:width] = nt(wd[...], jnp.concatenate(parts, axis=1))

    loop(0, pairs, decode)

    def slopes(r):
        t = lat[r + h, pl.ds(h, cols), :].astype(F32) * scale + shift
        sig = 0.5 * jnp.tanh(0.5 * t) + 0.5
        sact[r] = (sig * (1.0 + t * (1.0 - sig)) * gain).astype(BF16)

    loop(0, rows, slopes)

    pscale = color_column([0.5 / s for s in PIX_STD])
    pbias = color_column([((dbias[k] + 1.0) * 0.5 - PIX_MEAN[k]) * (1.0 / PIX_STD[k]) for k in range(3)])

    def pixels(p):
        c = tt[p, 0:24] + tt[p + 1, 24:48] + tt[p - 1, 48:72]
        x = (lane_taps(c) * pscale + pbias) * (lmask * valid_rows(2 * p))
        z = jnp.zeros((8, 256), F32)
        pixcol[p] = jnp.concatenate([pltpu.roll(x, 1, 1), x, pltpu.roll(x, 255, 1), z], axis=0).astype(BF16)

    loop(1, pairs - 1, pixels)

    def first(p):
        lhs = pixcol[pl.ds(p - 1, 3), :, 0:width].reshape(96, width)
        g, s = gelu_both(tn(lhs, w1[...]) + b1)
        m = cmask * valid_rows(2 * p)
        f = (g * m).astype(BF16)
        y1[p, :, 0:128] = f
        y1[p - 1, :, 128:192] = f[:, 0:64]
        y1[p + 1, :, 192:256] = f[:, 64:128]

        @pl.when((p >= 7) & (p < 25))
        def _():
            slope1[p - 7] = (s * m).astype(BF16)

    loop(1, pairs - 1, first)

    pr = iota((half, width), 0)
    pc = iota((half, width), 1) // 2
    pool = jnp.where(pr == pc, 0.25, 0.0).astype(BF16)

    def second(g):
        p0 = 2 + 4 * g
        x = y1[pl.ds(p0, 4)].reshape(4 * width, 256)
        pre = taps(jnp.dot(x, w2[...], preferred_element_type=F32), 128) + b2
        f, s = gelu_both(pre)
        for i in range(4):
            p = p0 + i
            m = cmask * valid_rows(2 * p)
            fi = (f[i * width : (i + 1) * width] * m).astype(BF16)
            f2[p] = fi
            half_sum = jnp.dot(pool, fi, preferred_element_type=F32)
            v = (half_sum + pltpu.roll(half_sum, 64, 1)).astype(BF16)
            k = 1 + 2 * g + i // 2
            if i % 2 == 0:
                yp[k, :, 0:64] = v[:, 0:64]
                yp[k - 1, :, 128:192] = v[:, 0:64]
            else:
                yp[k, :, 64:128] = v[:, 64:128]
                yp[k + 1, :, 192:256] = v[:, 64:128]

            @pl.when((p >= 6) & (p < 26))
            def _():
                feat2[p - 6] = fi
                slope2[p - 6] = (s[i * width : (i + 1) * width] * m).astype(BF16)

    loop(0, 7, second)

    def wide(g, w, src, stacked):
        k0 = stacked + 2 * g
        lhs = []
        for i in range(2):
            r = 2 * (k0 + i)
            lhs.append(jnp.concatenate([src[r - 1], src[r], src[r + 1], src[r + 2]], axis=1))
        return taps(jnp.dot(jnp.concatenate(lhs, axis=0), w[...], preferred_element_type=F32), 256)

    b33 = jnp.concatenate([b3, b3], axis=1)
    b44 = jnp.concatenate([b4, b4], axis=1)

    def third(g):
        k0 = 1 + 2 * g
        x = yp[pl.ds(k0, 2)].reshape(2 * half, 256)
        f, s = gelu_both(taps(jnp.dot(x, w3[...], preferred_element_type=F32), 256) + b33)
        for i in range(2):
            m = hmask * valid_rows(4 * (k0 + i))
            for q in range(2):
                r = 2 * (k0 + i) + q
                at = (slice(i * half, (i + 1) * half), slice(q * 128, (q + 1) * 128))
                f3[r] = (f[at] * m).astype(BF16)
                slope3[r] = (s[at] * m).astype(BF16)

    loop(0, 7, third)

    own = iota((half, 128), 0)
    omask = jnp.where((own >= h // 2) & (own < h // 2 + cols // 2), 1.0, 0.0).astype(F32)

    def fourth(g):
        k0 = 2 + 2 * g
        f, s = gelu_both(wide(g, w4, f3, 2) + b44)
        for i in range(2):
            m = hmask * valid_rows(4 * (k0 + i))
            for q in range(2):
                r = 2 * (k0 + i) + q
                at = (slice(i * half, (i + 1) * half), slice(q * 128, (q + 1) * 128))
                feat4[r - 4] = (f[at] * m).astype(BF16)
                slope4[r - 4] = (s[at] * m).astype(BF16)

                @pl.when((r >= 8) & (r < 24))
                def _():
                    fm[r - 8] = (f[at] * omask).astype(BF16)

    loop(0, 6, fourth)

    a = fm[...].reshape(16 * half, 128)
    gram[0:128] = tn(a, a)
    b = f2[8:24, h : h + cols, :].reshape(16 * cols, 128)
    gram[128:256] = tn(b, b)


def backward_kernel(
    dims,
    idx,
    totals,
    exlow,
    exhigh,
    slope1,
    feat2,
    slope2,
    slope3,
    feat4,
    slope4,
    sact,
    lat,
    stats,
    w4t,
    w3t,
    w2t,
    w1t,
    wdt,
    dxh,
    sums,
    loss,
    sw1,
    sw2,
    b4,
    b3,
    y2,
    tt,
    brgb,
):
    rows, cols, image_rows, image_cols, count = dims
    h = HALO
    width = cols + 2 * h
    half = width // 2
    npix = image_rows * image_cols
    row0 = idx[0] * rows - h
    col0 = idx[1] * cols - h

    def valid_rows(r):
        return jnp.where((row0 + r >= 0) & (row0 + r < image_rows), 1.0, 0.0).astype(F32)

    lane = iota((8, 256), 1)
    lmask = jnp.where((col0 + lane >= 0) & (col0 + lane < image_cols) & (lane < width), 1.0, 0.0)
    lmask = lmask.astype(F32)

    g1 = totals[128:256]
    g1 = g1 + pltpu.roll(pltpu.roll(g1, 64, 0), 64, 1)
    same = (iota((128, 128), 0) // 64) == (iota((128, 128), 1) // 64)
    gap1 = jnp.where(same, g1 * (1.0 / npix) - exlow[...], 0.0)
    gap2 = totals[0:128] * (4.0 / npix) - exhigh[...]
    value = jnp.sum(gap1 * gap1) * (0.5 / 4096.0) + jnp.sum(gap2 * gap2) * (1.0 / 16384.0)
    loss[...] = jnp.broadcast_to(value, loss.shape)
    for gap, sw in ((gap1, sw1), (gap2, sw2)):
        sym = 2.0 * (gap + gap.T)
        upper = sym.astype(BF16)
        sw[0:128] = upper
        sw[128:256] = (sym - upper.astype(F32)).astype(BF16)

    zrow = jnp.zeros((half, 128), BF16)
    b4[3] = zrow
    b4[28] = zrow
    tt[6] = jnp.zeros((72, 256), F32)
    tt[25] = jnp.zeros((72, 256), F32)
    tt[:, :, 128:256] = jnp.zeros((tt.shape[0], 72, 128), F32)

    def back4(g):
        x = feat4[pl.ds(4 * g, 4)].reshape(4 * half, 128)
        y = jnp.dot(jnp.concatenate([x, x], axis=1), sw2[...], preferred_element_type=F32)
        y = y * slope4[pl.ds(4 * g, 4)].reshape(4 * half, 128).astype(F32)
        b4[pl.ds(4 + 4 * g, 4)] = y.astype(BF16).reshape(4, half, 128)

    loop(0, 6, back4)

    def wide(k0, w, src, n):
        lhs = []
        for i in range(2):
            r = 2 * (k0 + i)
            lhs.append(jnp.concatenate([src[r - 1], src[r], src[r + 1], src[r + 2]], axis=1))
        return taps(jnp.dot(jnp.concatenate(lhs, axis=0), w[...], preferred_element_type=F32), n)

    def back3(g):
        k0 = 2 + 2 * g
        y = wide(k0, w4t, b4, 256)
        for i in range(2):
            for q in range(2):
                r = 2 * (k0 + i) + q
                part = y[i * half : (i + 1) * half, q * 128 : (q + 1) * 128]
                b3[r] = (part * slope3[r].astype(F32)).astype(BF16)

    loop(0, 6, back3)

    ur = iota((width, width), 0) // 2
    uc = iota((width, width), 1) % half
    spread = jnp.where(ur == uc, 0.25, 0.0).astype(BF16)
    first_half = iota((width, 128), 1) < 64

    def back2(g):
        k0 = 3 + 2 * g
        y = wide(k0, w3t, b3, 128)
        for i in range(2):
            gp = y[i * half : (i + 1) * half]
            upper = gp.astype(BF16)
            lower = (gp - upper.astype(F32)).astype(BF16)
            r = jnp.dot(spread, jnp.concatenate([upper, lower], axis=0), preferred_element_type=F32)
            rr = pltpu.roll(r, 64, 1)
            for q in range(2):
                p = 2 * (k0 + i) + q
                sp = jnp.where(first_half, r, rr) if q == 0 else jnp.where(first_half, rr, r)
                x = feat2[p - 6]
                gt = jnp.dot(jnp.concatenate([x, x], axis=1), sw1[...], preferred_element_type=F32)
                b = ((sp + gt) * slope2[p - 6].astype(F32)).astype(BF16)
                y2[p, :, 0:128] = b
                y2[p - 1, :, 128:192] = b[:, 0:64]
                y2[p + 1, :, 192:256] = b[:, 64:128]

    loop(0, 5, back2)

    def back1(g):
        p0 = 7 + 3 * g
        x = y2[pl.ds(p0, 3)].reshape(3 * width, 256)
        y = taps(jnp.dot(x, w2t[...], preferred_element_type=F32), 128)
        for i in range(3):
            b = (y[i * width : (i + 1) * width] * slope1[p0 + i - 7].astype(F32)).astype(BF16)
            tt[p0 + i, :, 0:width] = nt(w1t[...], b)

    loop(0, 6, back1)

    pscale = color_column([0.5 / s for s in PIX_STD])

    def colors(p):
        c = tt[p, 0:24] + tt[p + 1, 24:48] + tt[p - 1, 48:72]
        x = lane_taps(c) * pscale * (lmask * valid_rows(2 * p))
        parts = [pltpu.roll(x, 256 - h + d, 1)[:, 0:cols] for d in (1, 0, -1)]
        z = jnp.zeros((8, cols), F32)
        brgb[p] = jnp.concatenate(parts + [z], axis=0).astype(BF16)

    loop(7, 25, colors)

    mean, rstd = norm_values(stats[...], 128, count)
    offset = mean * rstd

    def last(p, carry):
        s, q = carry
        y = tn(brgb[pl.ds(p - 1, 3)].reshape(96, cols), wdt[...])
        for i in range(2):
            r = 2 * (p - 8) + i
            d = y[:, i * 128 : (i + 1) * 128] * sact[r].astype(F32)
            xh = lat[r].astype(F32) * rstd - offset
            dxh[r] = d.astype(BF16)
            s = s + jnp.sum(d.reshape(cols // 8, 8, 128), axis=0)
            q = q + jnp.sum((d * xh).reshape(cols // 8, 8, 128), axis=0)
        return s, q

    z = jnp.zeros((8, 128), F32)
    s, q = lax.fori_loop(8, 24, last, (z, z))
    sums[...] = jnp.broadcast_to(group_rows(s, q, 128), sums.shape)


def final_kernel(count, lat, dxh, stats, sums, out):
    mean, rstd = norm_values(stats[...], 128, count)
    n1, n2 = group_values(sums[...], 128, count)
    b = rstd * rstd * n2
    c = rstd * n1 - b * mean
    for r in range(out.shape[0]):
        y = dxh[r].astype(F32) * rstd - lat[r].astype(F32) * b - c
        out[r] = y.astype(BF16)


def full(shape):
    return pl.BlockSpec(shape, lambda *_: (0,) * len(shape))


def call(kernel, outs, scratch, args, kinds):
    specs = []
    for a, k in zip(args, kinds):
        if k == "s":
            specs.append(pl.BlockSpec(memory_space=pltpu.SMEM))
        elif k == "a":
            specs.append(pl.BlockSpec(memory_space=pl.ANY))
        else:
            specs.append(pl.BlockSpec(memory_space=pltpu.VMEM))
    return pl.pallas_call(
        kernel,
        out_shape=[jax.ShapeDtypeStruct(s, d) for s, d in outs],
        in_specs=specs,
        out_specs=[pl.BlockSpec(memory_space=pltpu.VMEM) for _ in outs],
        scratch_shapes=scratch,
        compiler_params=pltpu.CompilerParams(vmem_limit_bytes=56 * 1024 * 1024),
        interpret=INTERPRET,
    )(*args)


def local(
    latent,
    gain,
    bias,
    decoder_weight,
    decoder_bias,
    first_weight,
    first_bias,
    second_weight,
    second_bias,
    third_weight,
    third_bias,
    fourth_weight,
    fourth_bias,
    exemplar_low,
    exemplar_high,
):
    rows, cols, channels = latent.shape
    nrow, ncol = lax.axis_size("row"), lax.axis_size("col")
    n = nrow * ncol
    both = ("row", "col")
    h = HALO
    width = cols + 2 * h
    half = width // 2
    pairs = (rows + 2 * h) // 2
    image_rows, image_cols = rows * nrow, cols * ncol
    count = image_rows * image_cols * (channels // GROUPS)
    dims = (rows, cols, image_rows, image_cols, count)

    def shifted(x, dr, dc):
        perm = []
        for r in range(nrow):
            for c in range(ncol):
                a, b = r + dr, c + dc
                if 0 <= a < nrow and 0 <= b < ncol:
                    perm.append((r * ncol + c, a * ncol + b))
        return lax.ppermute(x, both, perm)

    up = shifted(latent[rows - h :], 1, 0)
    down = shifted(latent[:h], -1, 0)
    left = shifted(latent[:, cols - h :], 0, 1)
    right = shifted(latent[:, :h], 0, -1)
    ul = shifted(latent[rows - h :, cols - h :], 1, 1)
    ur = shifted(latent[rows - h :, :h], 1, -1)
    dl = shifted(latent[:h, cols - h :], -1, 1)
    dr = shifted(latent[:h, :h], -1, -1)

    def everyone(x):
        return lax.all_to_all(x, both, 0, 0, tiled=True)

    (mine,) = call(lambda *r: stats_kernel(n, *r), [((n, 128), F32)], [], [latent], "v")
    stats = everyone(mine)

    idx = jnp.stack([lax.axis_index("row"), lax.axis_index("col")]).astype(jnp.int32)
    vecs = jnp.concatenate(
        [
            gain,
            bias,
            first_bias,
            first_bias,
            second_bias,
            second_bias,
            third_bias,
            fourth_bias,
            jnp.zeros((256,), F32),
        ]
    ).reshape(8, 128)
    packed_order = (1, 2, 3, 0)
    row_order = (0, 1, 2, 3)
    wd = pack_narrow_out(decoder_weight)
    w1 = pack_narrow_in(first_weight)
    w2 = pack_stream(second_weight, packed_order)
    w3 = pack_stream(third_weight, packed_order)
    w4 = pack_stream(fourth_weight, row_order)
    w4t = pack_stream(flipped(fourth_weight), row_order)
    w3t = pack_stream(flipped(third_weight), row_order)
    w2t = pack_stream(flipped(second_weight), packed_order)
    w1t = pack_narrow_out(flipped(first_weight))
    wdt = pack_narrow_in(flipped(decoder_weight))

    states = call(
        lambda *r: forward_kernel(dims, *r),
        [
            ((256, 128), F32),
            ((18, width, 128), BF16),
            ((20, width, 128), BF16),
            ((20, width, 128), BF16),
            ((32, half, 128), BF16),
            ((24, half, 128), BF16),
            ((24, half, 128), BF16),
            ((rows, cols, 128), BF16),
        ],
        [
            pltpu.VMEM((2 * pairs, width, 128), BF16),
            pltpu.VMEM((pairs, 72, 256), F32),
            pltpu.VMEM((pairs, 32, 256), BF16),
            pltpu.VMEM((pairs, width, 256), BF16),
            pltpu.VMEM((pairs, width, 128), BF16),
            pltpu.VMEM((pairs // 2, half, 256), BF16),
            pltpu.VMEM((pairs, half, 128), BF16),
            pltpu.VMEM((16, half, 128), BF16),
            pltpu.SemaphoreType.DMA((9,)),
        ],
        [idx, decoder_bias, latent, up, down, left, right, ul, ur, dl, dr, stats, vecs, wd, w1, w2, w3, w4],
        "ss" + "a" * 9 + "v" * 7,
    )
    gram = states[0]
    mine = everyone(gram).reshape(n, 256 // n, 128).sum(axis=0)
    totals = everyone(jnp.broadcast_to(mine[None], (n, 256 // n, 128)).reshape(256, 128))
    exlow = jnp.tile(exemplar_low, (2, 2))

    dxh, sums, loss = call(
        lambda *r: backward_kernel(dims, *r),
        [((rows, cols, 128), BF16), ((n, 128), F32), ((8, 128), F32)],
        [
            pltpu.VMEM((256, 128), BF16),
            pltpu.VMEM((256, 128), BF16),
            pltpu.VMEM((pairs, half, 128), BF16),
            pltpu.VMEM((pairs, half, 128), BF16),
            pltpu.VMEM((pairs, width, 256), BF16),
            pltpu.VMEM((pairs, 72, 256), F32),
            pltpu.VMEM((pairs, 32, cols), BF16),
        ],
        [idx, totals, exlow, exemplar_high, *states[1:], latent, stats, w4t, w3t, w2t, w1t, wdt],
        "s" + "v" * 17,
    )
    sums = everyone(sums)

    step = 8
    blk = pl.BlockSpec((step, cols, 128), lambda i: (i, 0, 0))
    out = pl.pallas_call(
        lambda *r: final_kernel(count, *r),
        out_shape=jax.ShapeDtypeStruct((rows, cols, channels), BF16),
        grid=(rows // step,),
        in_specs=[blk, blk, full((n, 128)), full((n, 128))],
        out_specs=blk,
        interpret=INTERPRET,
    )(latent, dxh, stats, sums)
    return out, loss[0, 0]


def solution(mesh):
    placed = (P("row", "col", None),) + (P(),) * 14
    return jax.shard_map(
        local, mesh=mesh, in_specs=placed, out_specs=(P("row", "col", None), P()), check_vma=False
    )
```

```python
import jax
import jax.numpy as jnp
import numpy as np
from jax import lax
from jax.experimental import pallas as pl
from jax.experimental.pallas import tpu as pltpu
from jax.sharding import PartitionSpec as P

GROUPS = 32
EPS = 1e-05
PIX_MEAN = (0.485, 0.456, 0.406)
PIX_STD = (0.229, 0.224, 0.225)
HALO = 16
F32 = jnp.float32
BF16 = jnp.bfloat16
INTERPRET = False
VMEM_LIMIT = 40 * 1024 * 1024


def narrow_tables():
    out_fwd = np.zeros((2, 3, 3, 2, 4, 3, 3, 4), np.float32)
    out_bwd = np.zeros_like(out_fwd)
    in_fwd = np.zeros((2, 3, 3, 2, 4, 3, 3, 4), np.float32)
    in_bwd = np.zeros_like(in_fwd)
    for k, s in enumerate((0, -1, 1)):
        for dx in range(3):
            for q in range(2):
                for i in range(2):
                    dy = i - q - 2 * s + 1
                    if 0 <= dy < 3:
                        for c in range(3):
                            out_fwd[i, k, dx, q, c, dy, dx, c] = 1
                            out_bwd[i, k, dx, q, c, 2 - dy, 2 - dx, c] = 1
    for k, s in enumerate((-1, 0, 1)):
        for dx in range(3):
            for q in range(2):
                for i in range(2):
                    dy = 2 * s + i - q + 1
                    if 0 <= dy < 3:
                        for c in range(3):
                            in_fwd[q, k, dx, i, c, dy, dx, c] = 1
                            in_bwd[q, k, dx, i, c, 2 - dy, 2 - dx, c] = 1
    outs = np.concatenate([out_fwd.reshape(2, 72, 36), out_bwd.reshape(2, 72, 36)], 0)
    ins = np.concatenate([in_fwd.reshape(2, 3, 24, 36), in_bwd.reshape(2, 3, 24, 36)], 0)
    ins = np.pad(ins, ((0, 0), (0, 0), (0, 8), (0, 0))).reshape(4, 96, 36)
    return jnp.asarray(outs, BF16), jnp.asarray(ins, BF16)


def weights_kernel(dec, fst, w2r, w3r, w4r, outs, ins, wd, w1, w2, w3, w4, w4t, w3t, w2t, w1t, wdt):
    d, f = dec[...], fst[...]

    def place(t, x):
        return jnp.dot(t, x, preferred_element_type=F32)

    for i in range(2):
        wd[:, i * 128 : (i + 1) * 128] = place(outs[i], d).astype(BF16)
        wdt[:, i * 128 : (i + 1) * 128] = place(ins[2 + i], d).astype(BF16)
    w1[...] = jnp.concatenate([place(ins[0], f), place(ins[1], f)], axis=1).astype(BF16)
    w1t[...] = jnp.concatenate([place(outs[2], f), place(outs[3], f)], axis=1).astype(BF16)

    def tap(w, dy, dx, rows, cols):
        return w[dy, dx] if 0 <= dy < 3 else jnp.zeros((rows, cols), BF16)

    for k, j in enumerate((1, 2, 3, 0)):
        for dx in range(3):
            pair = [tap(w2r, j - q, dx, 64, 64) for q in range(2)]
            w2[k * 64 : (k + 1) * 64, dx * 128 : (dx + 1) * 128] = jnp.concatenate(pair, axis=1)
            pair = [tap(w2r, 2 - j + q, 2 - dx, 64, 64) for q in range(2)]
            w2t[k * 64 : (k + 1) * 64, dx * 128 : (dx + 1) * 128] = jnp.concatenate(pair, axis=0).T
            for q in range(2):
                at = dx * 256 + q * 128
                w3[k * 64 : (k + 1) * 64, at : at + 128] = tap(w3r, j - q, dx, 64, 128)
    for j in range(4):
        for dx in range(3):
            pair = [tap(w3r, 2 - j + q, 2 - dx, 64, 128) for q in range(2)]
            w3t[j * 128 : (j + 1) * 128, dx * 128 : (dx + 1) * 128] = jnp.concatenate(pair, axis=0).T
            for q in range(2):
                at = dx * 256 + q * 128
                w4[j * 128 : (j + 1) * 128, at : at + 128] = tap(w4r, j - q, dx, 128, 128)
                w4t[j * 128 : (j + 1) * 128, at : at + 128] = tap(w4r, 2 - j + q, 2 - dx, 128, 128).T


def iota(shape, axis):
    return lax.broadcasted_iota(jnp.int32, shape, axis)


def split3(x):
    hi = x.astype(BF16).astype(F32)
    mid = (x - hi).astype(BF16).astype(F32)
    lo = x - hi - mid
    r = iota((16, 128), 0)
    return jnp.where(r == 0, hi, jnp.where(r == 1, mid, jnp.where(r == 2, lo, 0.0))).astype(BF16)


def exact_dot(x, table):
    return jnp.sum(jnp.dot(split3(x), table, preferred_element_type=F32), axis=0, keepdims=True)


def group_rows(s, q):
    c = iota((128, 128), 0) // (128 // GROUPS)
    l = iota((128, 128), 1)
    g1 = jnp.where(l == c, 1.0, 0.0).astype(BF16)
    g2 = jnp.where(l == c + GROUPS, 1.0, 0.0).astype(BF16)
    s = jnp.sum(s, axis=0, keepdims=True)
    q = jnp.sum(q, axis=0, keepdims=True)
    return exact_dot(s, g1) + exact_dot(q, g2)


def group_values(rows, count):
    tot = jnp.sum(rows, axis=0, keepdims=True)
    l = iota((128, 256), 0)
    c = iota((128, 256), 1)
    want = (c % 128) // (128 // GROUPS) + GROUPS * (c // 128)
    e = jnp.where(l == want, 1.0, 0.0).astype(BF16)
    v = exact_dot(tot, e) * (1.0 / count)
    return v[:, 0:128], v[:, 128:256]


def norm_values(rows, count):
    mean, msq = group_values(rows, count)
    return mean, lax.rsqrt(msq - mean * mean + EPS)


def gelu_both(a):
    e = jnp.exp2(a * a * (-0.5 * 1.4426950408889634))
    t = 1.0 / (1.0 + jnp.abs(a) * (0.3275911 * 0.7071067811865476))
    poly = 0.5 * -1.453152027 + t * (0.5 * 1.061405429)
    poly = 0.5 * 1.421413741 + t * poly
    poly = 0.5 * -0.284496736 + t * poly
    q = t * (0.5 * 0.254829592 + t * poly) * e
    phi = jnp.where(a >= 0.0, 1.0 - q, q)
    return a * phi, phi + (a * 0.3989422804014327) * e


def pipelined(n, product, use, bufs):
    a, b = bufs
    product(0, a)
    steps = (n - 1) // 2

    def body(i):
        g = 2 * i
        product(g + 1, b)
        use(g, a)
        product(g + 2, a)
        use(g + 1, b)

    loop(0, steps, body)
    if n % 2 == 0:
        product(n - 1, b)
        use(n - 2, a)
        use(n - 1, b)
    else:
        use(n - 1, a)


def store_product(buf, x, w):
    m, n = x.shape[0], w.shape[1]
    buf[8 : 8 + m, 0:n] = jnp.dot(x, w, preferred_element_type=F32)
    buf[8 + m : 16 + m, 0:n] = jnp.zeros((8, n), F32)


def taps(buf, start, size, n, at=0, width=None):
    width = n if width is None else width
    lo = 8 + start
    return (
        buf[lo - 1 : lo - 1 + size, at : at + width]
        + buf[lo : lo + size, n + at : n + at + width]
        + buf[lo + 1 : lo + 1 + size, 2 * n + at : 2 * n + at + width]
    )


def lane_taps(c):
    return pltpu.roll(c[0:8], 1, 1) + c[8:16] + pltpu.roll(c[16:24], 255, 1)


def nt(a, b):
    return lax.dot_general(a, b, (((1,), (1,)), ((), ())), preferred_element_type=F32)


def tn(a, b):
    return lax.dot_general(a, b, (((0,), (0,)), ((), ())), preferred_element_type=F32)


def loop(lo, hi, body):
    lax.fori_loop(lo, hi, lambda i, c: (body(i), c)[1], 0)


def color_column(values):
    c = iota((8, 1), 0) % 4
    out = jnp.zeros((8, 1), F32)
    for k, v in enumerate(values):
        out = jnp.where(c == k, v, out)
    return out


def stats_kernel(n, x_ref, o_ref, down_out, up_out, right_out, left_out, dr_out, dl_out, ur_out, ul_out):
    h = HALO
    x_ref = x_ref.ready()
    rows, cols, channels = x_ref.shape
    down_out[...] = x_ref[rows - h : rows]
    up_out[...] = x_ref[0:h]
    right_out[...] = x_ref[:, cols - h : cols]
    left_out[...] = x_ref[:, 0:h]
    dr_out[...] = x_ref[rows - h : rows, cols - h : cols]
    dl_out[...] = x_ref[rows - h : rows, 0:h]
    ur_out[...] = x_ref[0:h, cols - h : cols]
    ul_out[...] = x_ref[0:h, 0:h]

    def body(r, carry):
        s, q = carry
        for i in range(4):
            x = x_ref[4 * r + i].astype(F32).reshape(cols // 8, 8, channels)
            s = s + jnp.sum(x, axis=0)
            q = q + jnp.sum(x * x, axis=0)
        return s, q

    z = jnp.zeros((8, channels), F32)
    s, q = lax.fori_loop(0, rows // 4, body, (z, z))
    o_ref[...] = jnp.broadcast_to(group_rows(s, q), (n, 128))


def forward_kernel(
    dims,
    idx,
    dbias,
    lat_hbm,
    up,
    down,
    left,
    right,
    ul,
    ur,
    dl,
    dr,
    stats,
    vecs,
    wd,
    w1,
    w2,
    w3,
    w4,
    gram,
    norm,
    o_slope1,
    o_feat2,
    o_slope2,
    o_slope3,
    o_feat4,
    o_slope4,
    o_sact,
    lat,
    tt,
    pixcol,
    y1,
    yp,
    f3,
    fm,
    cm,
    hm,
    om,
    pa,
    pb,
    sems,
):
    rows, cols, image_rows, image_cols, count = dims
    h = HALO
    width = cols + 2 * h
    half = width // 2
    pairs = (rows + 2 * h) // 2
    pieces = (
        (lat_hbm, lat.at[pl.ds(h, rows), pl.ds(h, cols)]),
        (up, lat.at[pl.ds(0, h), pl.ds(h, cols)]),
        (down, lat.at[pl.ds(h + rows, h), pl.ds(h, cols)]),
        (left, lat.at[pl.ds(h, rows), pl.ds(0, h)]),
        (right, lat.at[pl.ds(h, rows), pl.ds(h + cols, h)]),
        (ul, lat.at[pl.ds(0, h), pl.ds(0, h)]),
        (ur, lat.at[pl.ds(0, h), pl.ds(h + cols, h)]),
        (dl, lat.at[pl.ds(h + rows, h), pl.ds(0, h)]),
        (dr, lat.at[pl.ds(h + rows, h), pl.ds(h + cols, h)]),
    )
    copies = [pltpu.make_async_copy(a, b, sems.at[i]) for i, (a, b) in enumerate(pieces)]
    for c in copies:
        c.start()
    slope1, feat2, slope2, slope3 = o_slope1.ref, o_feat2.ref, o_slope2.ref, o_slope3.ref
    feat4, slope4, sact = o_feat4.ref, o_slope4.ref, o_sact.ref

    pa[0:8] = jnp.zeros((8, pa.shape[1]), F32)
    pb[0:8] = jnp.zeros((8, pb.shape[1]), F32)
    tt[:, :, 128:256] = jnp.zeros((pairs, 72, 128), F32)
    pixcol[0] = jnp.zeros((32, 256), BF16)
    pixcol[pairs - 1] = jnp.zeros((32, 256), BF16)
    yp[1, :, 192:256] = jnp.zeros((half, 64), BF16)
    yp[pairs // 2 - 2, :, 128:192] = jnp.zeros((half, 64), BF16)

    row0 = idx[0] * rows - h
    col0 = idx[1] * cols - h

    def valid_rows(r):
        return jnp.where((row0 + r >= 0) & (row0 + r < image_rows), 1.0, 0.0).astype(F32)

    def valid_lanes(r):
        return jnp.full((1, 128), valid_rows(r), F32).astype(BF16)

    def col_mask(n, step, lanes):
        c = col0 + step * iota((n, lanes), 0)
        return jnp.where((c >= 0) & (c < image_cols), 1.0, 0.0).astype(BF16)

    cm[...] = col_mask(width, 1, 128)
    hm[...] = col_mask(half, 2, 128)
    own = iota((half, 128), 0)
    om[...] = jnp.where((own >= h // 2) & (own < h // 2 + cols // 2), 1.0, 0.0).astype(BF16)
    lane = iota((8, 256), 1)
    lmask = jnp.where((col0 + lane >= 0) & (col0 + lane < image_cols) & (lane < width), 1.0, 0.0)
    lmask = lmask.astype(F32)

    mean, rstd = norm_values(stats[...], count)
    norm[0:1] = mean
    norm[1:2] = rstd
    gain = vecs[0:1]
    scale = rstd * gain
    shift = vecs[1:2] - mean * scale
    b1, b2, b3, b4 = vecs[2:3], vecs[3:4], vecs[4:5], vecs[5:6]

    for c in copies:
        c.wait()
    wd = wd.ready()

    half_scale, half_shift = 0.5 * scale, 0.5 * shift

    def decode(p, own_rows):
        parts = []
        m = cm[...] * valid_lanes(2 * p)
        for i in range(2):
            t2 = lat[2 * p + i].astype(F32) * half_scale + half_shift
            th = jnp.tanh(t2)
            ts = t2 * th + t2
            parts.append(ts.astype(BF16) * m)
            if own_rows:
                th, t2 = th[h : h + cols], t2[h : h + cols]
                sl = (0.5 + 0.5 * th) * (1.0 + t2 * (1.0 - th))
                sact[2 * p + i - h] = (sl * gain).astype(BF16)
        tt[p, :, 0:width] = nt(wd[...], jnp.concatenate(parts, axis=1))

    def decode_two(p, own_rows):
        decode(p, own_rows)
        decode(p + 1, own_rows)

    loop(0, 4, lambda i: decode_two(2 * i, False))
    loop(4, 12, lambda i: decode_two(2 * i, True))
    loop(12, 16, lambda i: decode_two(2 * i, False))
    o_sact.send()
    w1, w2, w3, w4 = w1.ready(), w2.ready(), w3.ready(), w4.ready()

    pscale = color_column([0.5 / s for s in PIX_STD])
    pbias = color_column([((dbias[k] + 1.0) * 0.5 - PIX_MEAN[k]) * (1.0 / PIX_STD[k]) for k in range(3)])

    def pixels(p):
        c = tt[p, 0:24] + tt[p + 1, 24:48] + tt[p - 1, 48:72]
        x = (lane_taps(c) * pscale + pbias) * (lmask * valid_rows(2 * p))
        z = jnp.zeros((8, 256), F32)
        pixcol[p] = jnp.concatenate([pltpu.roll(x, 1, 1), x, pltpu.roll(x, 255, 1), z], axis=0).astype(BF16)

    def pixels_three(i):
        for k in range(3):
            pixels(1 + 3 * i + k)

    loop(0, (pairs - 2) // 3, pixels_three)

    def first_product(g, buf):
        for i in range(2):
            p = 1 + 2 * g + i
            lhs = pixcol[pl.ds(p - 1, 3), :, 0:width].reshape(96, width)
            buf[8 + i * width : 8 + (i + 1) * width, 0:128] = tn(lhs, w1[...])

    def first_use(g, buf):
        for i in range(2):
            p = 1 + 2 * g + i
            gl, sl = gelu_both(buf[8 + i * width : 8 + (i + 1) * width, 0:128] + b1)
            m = cm[...] * valid_lanes(2 * p)
            f = gl.astype(BF16) * m
            y1[p, :, 0:128] = f
            y1[p - 1, :, 128:192] = f[:, 0:64]
            y1[p + 1, :, 192:256] = f[:, 64:128]
            slope1[p] = sl.astype(BF16) * m

    pipelined((pairs - 2) // 2, first_product, first_use, (pa, pb))
    o_slope1.send()

    pr = iota((half, width), 0)
    pc = iota((half, width), 1) // 2
    pool = jnp.where(pr == pc, 0.25, 0.0).astype(BF16)

    def second_product(g, buf):
        store_product(buf, y1[pl.ds(2 + 4 * g, 4)].reshape(4 * width, 256), w2[...])

    def second_use(g, buf):
        p0 = 2 + 4 * g
        for i in range(4):
            p = p0 + i
            f, sl = gelu_both(taps(buf, i * width, width, 128) + b2)
            m = cm[...] * valid_lanes(2 * p)
            fi = f.astype(BF16) * m
            feat2[p] = fi
            slope2[p] = sl.astype(BF16) * m
            half_sum = jnp.dot(pool, fi, preferred_element_type=F32)
            v = (half_sum + pltpu.roll(half_sum, 64, 1)).astype(BF16)
            k = 1 + 2 * g + i // 2
            if i % 2 == 0:
                yp[k, :, 0:64] = v[:, 0:64]
                yp[k - 1, :, 128:192] = v[:, 0:64]
            else:
                yp[k, :, 64:128] = v[:, 64:128]
                yp[k + 1, :, 192:256] = v[:, 64:128]

    pipelined(7, second_product, second_use, (pa, pb))
    o_feat2.send()
    o_slope2.send()

    def third_product(g, buf):
        store_product(buf, yp[pl.ds(1 + 2 * g, 2)].reshape(2 * half, 256), w3[...])

    def wide_use(k0, buf, n, bias, keep):
        for i in range(n):
            m = hm[...] * valid_lanes(4 * (k0 + i))
            for q in range(2):
                f, sl = gelu_both(taps(buf, i * half, half, 256, q * 128, 128) + bias)
                keep(2 * (k0 + i) + q, f.astype(BF16) * m, sl.astype(BF16) * m)

    def third_keep(r, f, sl):
        f3[r] = f
        slope3[r] = sl

    pipelined(7, third_product, lambda g, buf: wide_use(1 + 2 * g, buf, 2, b3, third_keep), (pa, pb))
    o_slope3.send()

    def fourth_product(g, buf):
        lhs = []
        for i in range(4):
            r = 2 * (2 + 4 * g + i)
            lhs.append(jnp.concatenate([f3[r - 1], f3[r], f3[r + 1], f3[r + 2]], axis=1))
        store_product(buf, jnp.concatenate(lhs, axis=0), w4[...])

    def fourth_keep(r, f, sl):
        feat4[r] = f
        slope4[r] = sl
        fm[r] = f * om[...]

    pipelined(3, fourth_product, lambda g, buf: wide_use(2 + 4 * g, buf, 4, b4, fourth_keep), (pa, pb))
    o_feat4.send()
    o_slope4.send()

    a = fm[8:24].reshape(16 * half, 128)
    gram[0:128] = tn(a, a)
    b = feat2[8:24, h : h + cols, :].reshape(16 * cols, 128)
    gram[128:256] = tn(b, b)


def backward_kernel(
    dims,
    idx,
    totals,
    exlow,
    exhigh,
    slope1,
    feat2,
    slope2,
    slope3,
    feat4,
    slope4,
    sact,
    lat,
    norm,
    w4t,
    w3t,
    w2t,
    w1t,
    wdt,
    o_dxh,
    sums,
    loss,
    sw1,
    sw2,
    b4,
    b3,
    y2,
    tt,
    brgb,
    pa,
    pb,
):
    rows, cols, image_rows, image_cols, count = dims
    h = HALO
    width = cols + 2 * h
    half = width // 2
    npix = image_rows * image_cols
    row0 = idx[0] * rows - h
    col0 = idx[1] * cols - h

    def valid_rows(r):
        return jnp.where((row0 + r >= 0) & (row0 + r < image_rows), 1.0, 0.0).astype(F32)

    lane = iota((8, 256), 1)
    lmask = jnp.where((col0 + lane >= 0) & (col0 + lane < image_cols) & (lane < width), 1.0, 0.0)
    lmask = lmask.astype(F32)

    g1 = totals[128:256]
    g1 = g1 + pltpu.roll(pltpu.roll(g1, 64, 0), 64, 1)
    same = (iota((128, 128), 0) // 64) == (iota((128, 128), 1) // 64)
    gap1 = jnp.where(same, g1 * (1.0 / npix) - exlow[...], 0.0)
    gap2 = totals[0:128] * (4.0 / npix) - exhigh[...]
    value = jnp.sum(gap1 * gap1) * (0.5 / 4096.0) + jnp.sum(gap2 * gap2) * (1.0 / 16384.0)
    loss[...] = jnp.broadcast_to(value, loss.shape)
    for gap, sw in ((gap1, sw1), (gap2, sw2)):
        sym = 2.0 * (gap + gap.T)
        upper = sym.astype(BF16)
        sw[0:128] = upper
        sw[128:256] = (sym - upper.astype(F32)).astype(BF16)

    pa[0:8] = jnp.zeros((8, pa.shape[1]), F32)
    pb[0:8] = jnp.zeros((8, pb.shape[1]), F32)
    zrow = jnp.zeros((half, 128), BF16)
    b4[3] = zrow
    b4[28] = zrow
    tt[6] = jnp.zeros((72, 256), F32)
    tt[25] = jnp.zeros((72, 256), F32)
    tt[:, :, 128:256] = jnp.zeros((tt.shape[0], 72, 128), F32)

    def back4(g):
        r0 = 4 + 4 * g
        x = feat4[pl.ds(r0, 4)].reshape(4 * half, 128)
        y = jnp.dot(jnp.concatenate([x, x], axis=1), sw2[...], preferred_element_type=F32)
        y = y * slope4[pl.ds(r0, 4)].reshape(4 * half, 128).astype(F32)
        b4[pl.ds(r0, 4)] = y.astype(BF16).reshape(4, half, 128)

    feat4, slope4 = feat4.ready(), slope4.ready()
    loop(0, 6, back4)
    slope3, w4t, w3t = slope3.ready(), w4t.ready(), w3t.ready()

    def wide(k0, n, src, w, buf):
        lhs = []
        for i in range(n):
            r = 2 * (k0 + i)
            lhs.append(jnp.concatenate([src[r - 1], src[r], src[r + 1], src[r + 2]], axis=1))
        store_product(buf, jnp.concatenate(lhs, axis=0), w[...])

    def back3(g, buf):
        k0 = 2 + 4 * g
        for i in range(4):
            for q in range(2):
                r = 2 * (k0 + i) + q
                part = taps(buf, i * half, half, 256, q * 128, 128)
                b3[r] = (part * slope3[r].astype(F32)).astype(BF16)

    pipelined(3, lambda g, buf: wide(2 + 4 * g, 4, b4, w4t, buf), back3, (pa, pb))
    feat2, slope2 = feat2.ready(), slope2.ready()

    ur = iota((width, width), 0) // 2
    uc = iota((width, width), 1) % half
    spread = jnp.where(ur == uc, 0.25, 0.0).astype(BF16)
    first_half = iota((width, 128), 1) < 64

    def back2(g, buf):
        k0 = 3 + 2 * g
        for i in range(2):
            gp = taps(buf, i * half, half, 128)
            upper = gp.astype(BF16)
            lower = (gp - upper.astype(F32)).astype(BF16)
            r = jnp.dot(spread, jnp.concatenate([upper, lower], axis=0), preferred_element_type=F32)
            rr = pltpu.roll(r, 64, 1)
            for q in range(2):
                p = 2 * (k0 + i) + q
                sp = jnp.where(first_half, r, rr) if q == 0 else jnp.where(first_half, rr, r)
                x = feat2[p]
                gt = jnp.dot(jnp.concatenate([x, x], axis=1), sw1[...], preferred_element_type=F32)
                b = ((sp + gt) * slope2[p].astype(F32)).astype(BF16)
                y2[p, :, 0:128] = b
                y2[p - 1, :, 128:192] = b[:, 0:64]
                y2[p + 1, :, 192:256] = b[:, 64:128]

    pipelined(5, lambda g, buf: wide(3 + 2 * g, 2, b3, w3t, buf), back2, (pa, pb))
    slope1, w2t, w1t = slope1.ready(), w2t.ready(), w1t.ready()

    def back1_product(g, buf):
        store_product(buf, y2[pl.ds(7 + 3 * g, 3)].reshape(3 * width, 256), w2t[...])

    def back1(g, buf):
        for i in range(3):
            p = 7 + 3 * g + i
            b = (taps(buf, i * width, width, 128) * slope1[p].astype(F32)).astype(BF16)
            tt[p, :, 0:width] = nt(w1t[...], b)

    pipelined(6, back1_product, back1, (pa, pb))

    pscale = color_column([0.5 / s for s in PIX_STD])

    def colors(p):
        c = tt[p, 0:24] + tt[p + 1, 24:48] + tt[p - 1, 48:72]
        x = lane_taps(c) * pscale * (lmask * valid_rows(2 * p))
        parts = [pltpu.roll(x, 256 - h + d, 1)[:, 0:cols] for d in (1, 0, -1)]
        z = jnp.zeros((8, cols), F32)
        brgb[p] = jnp.concatenate(parts + [z], axis=0).astype(BF16)

    def colors_three(i):
        for k in range(3):
            colors(7 + 3 * i + k)

    loop(0, 6, colors_three)

    mean, rstd = norm[0:1], norm[1:2]
    offset = mean * rstd
    sact, lat, wdt = sact.ready(), lat.ready(), wdt.ready()
    dxh = o_dxh.ref

    def last_two(i, carry):
        return last(9 + 2 * i, last(8 + 2 * i, carry))

    def last(p, carry):
        s, q = carry
        y = tn(brgb[pl.ds(p - 1, 3)].reshape(96, cols), wdt[...])
        for i in range(2):
            r = 2 * (p - 8) + i
            d = y[:, i * 128 : (i + 1) * 128] * sact[r].astype(F32)
            xh = lat[r].astype(F32) * rstd - offset
            dxh[r] = d.astype(BF16)
            s = s + jnp.sum(d.reshape(cols // 8, 8, 128), axis=0)
            q = q + jnp.sum((d * xh).reshape(cols // 8, 8, 128), axis=0)
        return s, q

    z = jnp.zeros((8, 128), F32)
    s, q = lax.fori_loop(0, 8, last_two, (z, z))
    o_dxh.send()
    sums[...] = jnp.broadcast_to(group_rows(s, q), sums.shape)


def final_kernel(count, lat, dxh, norm, sums, out, coef):
    @pl.when(pl.program_id(0) == 0)
    def _():
        mean, rstd = norm[0:1], norm[1:2]
        n1, n2 = group_values(sums[...], count)
        b = rstd * rstd * n2
        coef[0:1] = rstd
        coef[1:2] = b
        coef[2:3] = rstd * n1 - b * mean

    a, b, c = coef[0:1], coef[1:2], coef[2:3]

    def body(r):
        out[r] = (dxh[r].astype(F32) * a - lat[r].astype(F32) * b - c).astype(BF16)

    loop(0, out.shape[0], body)


def full(shape):
    return pl.BlockSpec(shape, lambda *_: (0,) * len(shape))


def placed_at(x, space):
    return x if INTERPRET else pltpu.with_memory_space_constraint(x, space)


class Arriving:
    def __init__(self, src, dst, sem):
        self.dst = dst
        self.copy = pltpu.make_async_copy(src, dst, sem)
        self.copy.start()

    def ready(self):
        self.copy.wait()
        return self.dst


class Leaving:
    def __init__(self, src, dst, sem):
        self.ref = src
        self.copy = pltpu.make_async_copy(src, dst, sem)

    def send(self):
        self.copy.start()


def call(kernel, outs, scratch, args, kinds, out_kinds):
    spaces = {"s": pltpu.SMEM, "a": pl.ANY, "d": pl.ANY, "v": pltpu.VMEM, "m": pltpu.VMEM}
    late_in = [i for i, k in enumerate(kinds) if k == "d"]
    late_out = [i for i, k in enumerate(out_kinds) if k == "d"]
    buffers = [pltpu.VMEM(args[i].shape, args[i].dtype) for i in late_in]
    buffers += [pltpu.VMEM(*outs[i]) for i in late_out]
    sems = [pltpu.SemaphoreType.DMA((len(buffers),))] if buffers else []

    def body(*refs):
        refs = list(refs)
        n_in, n_out = len(args), len(outs)
        ins, results, rest = refs[:n_in], refs[n_in : n_in + n_out], refs[n_in + n_out :]
        own, extra = rest[: len(scratch)], rest[len(scratch) :]
        leaving = []
        for j, i in enumerate(late_in):
            ins[i] = Arriving(ins[i], extra[j], extra[-1].at[j])
        for j, i in enumerate(late_out):
            k = len(late_in) + j
            results[i] = Leaving(extra[k], results[i], extra[-1].at[k])
            leaving.append(results[i])
        kernel(*ins, *results, *own)
        for x in leaving:
            x.copy.wait()

    return pl.pallas_call(
        body,
        out_shape=[jax.ShapeDtypeStruct(s, d) if INTERPRET else pltpu.HBM(s, d) for s, d in outs],
        in_specs=[pl.BlockSpec(memory_space=spaces[k]) for k in kinds],
        out_specs=[pl.BlockSpec(memory_space=spaces[k]) for k in out_kinds],
        scratch_shapes=list(scratch) + buffers + sems,
        compiler_params=pltpu.CompilerParams(vmem_limit_bytes=VMEM_LIMIT),
        interpret=INTERPRET,
    )(*[a if k == "s" else placed_at(a, pltpu.VMEM if k == "m" else pltpu.HBM) for a, k in zip(args, kinds)])


def local(
    latent,
    gain,
    bias,
    decoder_weight,
    decoder_bias,
    first_weight,
    first_bias,
    second_weight,
    second_bias,
    third_weight,
    third_bias,
    fourth_weight,
    fourth_bias,
    exemplar_low,
    exemplar_high,
):
    rows, cols, channels = latent.shape
    nrow, ncol = lax.axis_size("row"), lax.axis_size("col")
    n = nrow * ncol
    both = ("row", "col")
    h = HALO
    width = cols + 2 * h
    half = width // 2
    pairs = (rows + 2 * h) // 2
    image_rows, image_cols = rows * nrow, cols * ncol
    count = image_rows * image_cols * (channels // GROUPS)
    dims = (rows, cols, image_rows, image_cols, count)

    def shifted(x, dr, dc):
        perm = []
        for r in range(nrow):
            for c in range(ncol):
                a, b = r + dr, c + dc
                if 0 <= a < nrow and 0 <= b < ncol:
                    perm.append((r * ncol + c, a * ncol + b))
        return lax.ppermute(x, both, perm)

    def everyone(x):
        return lax.all_to_all(x, both, 0, 0, tiled=True)

    mine, *edges = call(
        lambda *r: stats_kernel(n, *r),
        [((n, 128), F32)]
        + [((h, cols, 128), BF16)] * 2
        + [((rows, h, 128), BF16)] * 2
        + [((h, h, 128), BF16)] * 4,
        [],
        [latent],
        "d",
        "v" * 9,
    )
    stats = everyone(mine)
    moves = ((1, 0), (-1, 0), (0, 1), (0, -1), (1, 1), (1, -1), (-1, 1), (-1, -1))
    halos = [shifted(x, *m) for x, m in zip(edges, moves)]

    idx = jnp.stack([lax.axis_index("row"), lax.axis_index("col")]).astype(jnp.int32)
    vecs = jnp.concatenate(
        [
            gain,
            bias,
            first_bias,
            first_bias,
            second_bias,
            second_bias,
            third_bias,
            fourth_bias,
            jnp.zeros((256,), F32),
        ]
    ).reshape(8, 128)
    dec = jnp.pad(jnp.transpose(decoder_weight, (0, 1, 3, 2)), ((0, 0), (0, 0), (0, 1), (0, 0)))
    fst = jnp.pad(first_weight, ((0, 0), (0, 0), (0, 1), (0, 0)))
    wd, w1, w2, w3, w4, w4t, w3t, w2t, w1t, wdt = call(
        weights_kernel,
        [
            ((72, 256), BF16),
            ((96, 128), BF16),
            ((256, 384), BF16),
            ((256, 768), BF16),
            ((512, 768), BF16),
            ((512, 768), BF16),
            ((512, 384), BF16),
            ((256, 384), BF16),
            ((72, 128), BF16),
            ((96, 256), BF16),
        ],
        [],
        [
            dec.reshape(36, 128),
            fst.reshape(36, 64),
            second_weight,
            third_weight,
            fourth_weight,
            *narrow_tables(),
        ],
        "v" * 7,
        "v" * 10,
    )

    states = call(
        lambda *r: forward_kernel(dims, *r),
        [
            ((256, 128), F32),
            ((8, 128), F32),
            ((pairs, width, 128), BF16),
            ((pairs, width, 128), BF16),
            ((pairs, width, 128), BF16),
            ((pairs, half, 128), BF16),
            ((pairs, half, 128), BF16),
            ((pairs, half, 128), BF16),
            ((rows, cols, 128), BF16),
        ],
        [
            pltpu.VMEM((2 * pairs, width, 128), BF16),
            pltpu.VMEM((pairs, 72, 256), F32),
            pltpu.VMEM((pairs, 32, 256), BF16),
            pltpu.VMEM((pairs, width, 256), BF16),
            pltpu.VMEM((pairs // 2, half, 256), BF16),
            pltpu.VMEM((pairs, half, 128), BF16),
            pltpu.VMEM((pairs, half, 128), BF16),
            pltpu.VMEM((width, 128), BF16),
            pltpu.VMEM((half, 128), BF16),
            pltpu.VMEM((half, 128), BF16),
            pltpu.VMEM((4 * width + 16, 768), F32),
            pltpu.VMEM((4 * width + 16, 768), F32),
            pltpu.SemaphoreType.DMA((9,)),
        ],
        [idx, decoder_bias, latent, *halos, stats, vecs, wd, w1, w2, w3, w4],
        "ssa" + "mm" + "a" * 6 + "mv" + "d" * 5,
        "vv" + "d" * 7,
    )
    gram, norm = states[:2]
    mine = everyone(gram).reshape(n, 256 // n, 128).sum(axis=0)
    totals = everyone(jnp.broadcast_to(mine[None], (n, 256 // n, 128)).reshape(256, 128))
    exlow = jnp.tile(exemplar_low, (2, 2))

    dxh, sums, loss = call(
        lambda *r: backward_kernel(dims, *r),
        [((rows, cols, 128), BF16), ((n, 128), F32), ((8, 128), F32)],
        [
            pltpu.VMEM((256, 128), BF16),
            pltpu.VMEM((256, 128), BF16),
            pltpu.VMEM((pairs, half, 128), BF16),
            pltpu.VMEM((pairs, half, 128), BF16),
            pltpu.VMEM((pairs, width, 256), BF16),
            pltpu.VMEM((pairs, 72, 256), F32),
            pltpu.VMEM((pairs, 32, cols), BF16),
            pltpu.VMEM((4 * width + 16, 768), F32),
            pltpu.VMEM((4 * width + 16, 768), F32),
        ],
        [idx, totals, exlow, exemplar_high, *states[2:], latent, norm, w4t, w3t, w2t, w1t, wdt],
        "smvv" + "d" * 8 + "v" + "d" * 5,
        "dvv",
    )
    sums = everyone(sums)

    step = 8
    blk = pl.BlockSpec((step, cols, 128), lambda i: (i, 0, 0))
    whole = pl.BlockSpec(memory_space=pltpu.VMEM)
    out = pl.pallas_call(
        lambda *r: final_kernel(count, *r),
        out_shape=jax.ShapeDtypeStruct((rows, cols, channels), BF16) if INTERPRET else pltpu.HBM((rows, cols, channels), BF16),
        grid=(rows // step,),
        in_specs=[blk, blk, whole, whole],
        out_specs=blk,
        scratch_shapes=[pltpu.VMEM((8, 128), F32)],
        compiler_params=pltpu.CompilerParams(vmem_limit_bytes=VMEM_LIMIT),
        interpret=INTERPRET,
    )(placed_at(latent, pltpu.HBM), placed_at(dxh, pltpu.HBM), placed_at(norm, pltpu.HBM), placed_at(sums, pltpu.VMEM))
    return out, loss[0, 0]


def solution(mesh):
    placed = (P("row", "col", None),) + (P(),) * 14
    return jax.shard_map(
        local, mesh=mesh, in_specs=placed, out_specs=(P("row", "col", None), P()), check_vma=False
    )
```

```python
import jax
import jax.numpy as jnp
import numpy as np
from jax import lax
from jax.experimental import pallas as pl
from jax.experimental.pallas import tpu as pltpu
from jax.sharding import PartitionSpec as P

GROUPS = 32
EPS = 1e-05
PIX_MEAN = (0.485, 0.456, 0.406)
PIX_STD = (0.229, 0.224, 0.225)
HALO = 16
F32 = jnp.float32
BF16 = jnp.bfloat16
INTERPRET = False
VMEM_LIMIT = 40 * 1024 * 1024


def narrow_tables():
    out_fwd = np.zeros((2, 3, 3, 2, 4, 3, 3, 4), np.float32)
    out_bwd = np.zeros_like(out_fwd)
    in_fwd = np.zeros((2, 3, 3, 2, 4, 3, 3, 4), np.float32)
    in_bwd = np.zeros_like(in_fwd)
    for k, s in enumerate((0, -1, 1)):
        for dx in range(3):
            for q in range(2):
                for i in range(2):
                    dy = i - q - 2 * s + 1
                    if 0 <= dy < 3:
                        for c in range(3):
                            out_fwd[i, k, dx, q, c, dy, dx, c] = 1
                            out_bwd[i, k, dx, q, c, 2 - dy, 2 - dx, c] = 1
    for k, s in enumerate((-1, 0, 1)):
        for dx in range(3):
            for q in range(2):
                for i in range(2):
                    dy = 2 * s + i - q + 1
                    if 0 <= dy < 3:
                        for c in range(3):
                            in_fwd[q, k, dx, i, c, dy, dx, c] = 1
                            in_bwd[q, k, dx, i, c, 2 - dy, 2 - dx, c] = 1
    outs = np.concatenate([out_fwd.reshape(2, 72, 36), out_bwd.reshape(2, 72, 36)], 0)
    ins = np.concatenate([in_fwd.reshape(2, 3, 24, 36), in_bwd.reshape(2, 3, 24, 36)], 0)
    ins = np.pad(ins, ((0, 0), (0, 0), (0, 8), (0, 0))).reshape(4, 96, 36)
    return jnp.asarray(outs, BF16), jnp.asarray(ins, BF16)


def weights_kernel(dec, fst, w2r, w3r, w4r, outs, ins, wd, w1, w2, w3, w4, w4t, w3t, w2t, w1t, wdt):
    d, f = dec[...], fst[...]

    def place(t, x):
        return jnp.dot(t, x, preferred_element_type=F32)

    for i in range(2):
        wd[:, i * 128 : (i + 1) * 128] = place(outs[i], d).astype(BF16)
        wdt[:, i * 128 : (i + 1) * 128] = place(ins[2 + i], d).astype(BF16)
    w1[...] = jnp.concatenate([place(ins[0], f), place(ins[1], f)], axis=1).astype(BF16)
    w1t[...] = jnp.concatenate([place(outs[2], f), place(outs[3], f)], axis=1).astype(BF16)

    def tap(w, dy, dx, rows, cols):
        return w[dy, dx] if 0 <= dy < 3 else jnp.zeros((rows, cols), BF16)

    for k, j in enumerate((1, 2, 3, 0)):
        for dx in range(3):
            pair = [tap(w2r, j - q, dx, 64, 64) for q in range(2)]
            w2[k * 64 : (k + 1) * 64, dx * 128 : (dx + 1) * 128] = jnp.concatenate(pair, axis=1)
            pair = [tap(w2r, 2 - j + q, 2 - dx, 64, 64) for q in range(2)]
            w2t[k * 64 : (k + 1) * 64, dx * 128 : (dx + 1) * 128] = jnp.concatenate(pair, axis=0).T
            for q in range(2):
                at = dx * 256 + q * 128
                w3[k * 64 : (k + 1) * 64, at : at + 128] = tap(w3r, j - q, dx, 64, 128)
    for j in range(4):
        for dx in range(3):
            pair = [tap(w3r, 2 - j + q, 2 - dx, 64, 128) for q in range(2)]
            w3t[j * 128 : (j + 1) * 128, dx * 128 : (dx + 1) * 128] = jnp.concatenate(pair, axis=0).T
            for q in range(2):
                at = dx * 256 + q * 128
                w4[j * 128 : (j + 1) * 128, at : at + 128] = tap(w4r, j - q, dx, 128, 128)
                w4t[j * 128 : (j + 1) * 128, at : at + 128] = tap(w4r, 2 - j + q, 2 - dx, 128, 128).T


def iota(shape, axis):
    return lax.broadcasted_iota(jnp.int32, shape, axis)


def split3(x):
    hi = x.astype(BF16).astype(F32)
    mid = (x - hi).astype(BF16).astype(F32)
    lo = x - hi - mid
    r = iota((16, 128), 0)
    return jnp.where(r == 0, hi, jnp.where(r == 1, mid, jnp.where(r == 2, lo, 0.0))).astype(BF16)


def exact_dot(x, table):
    return jnp.sum(jnp.dot(split3(x), table, preferred_element_type=F32), axis=0, keepdims=True)


def group_rows(s, q):
    c = iota((128, 128), 0) // (128 // GROUPS)
    l = iota((128, 128), 1)
    g1 = jnp.where(l == c, 1.0, 0.0).astype(BF16)
    g2 = jnp.where(l == c + GROUPS, 1.0, 0.0).astype(BF16)
    s = jnp.sum(s, axis=0, keepdims=True)
    q = jnp.sum(q, axis=0, keepdims=True)
    return exact_dot(s, g1) + exact_dot(q, g2)


def group_values(rows, count):
    tot = jnp.sum(rows, axis=0, keepdims=True)
    l = iota((128, 256), 0)
    c = iota((128, 256), 1)
    want = (c % 128) // (128 // GROUPS) + GROUPS * (c // 128)
    e = jnp.where(l == want, 1.0, 0.0).astype(BF16)
    v = exact_dot(tot, e) * (1.0 / count)
    return v[:, 0:128], v[:, 128:256]


def norm_values(rows, count):
    mean, msq = group_values(rows, count)
    return mean, lax.rsqrt(msq - mean * mean + EPS)


def gelu_both(a):
    e = jnp.exp2(a * a * (-0.5 * 1.4426950408889634))
    t = 1.0 / (1.0 + jnp.abs(a) * (0.3275911 * 0.7071067811865476))
    poly = 0.5 * -1.453152027 + t * (0.5 * 1.061405429)
    poly = 0.5 * 1.421413741 + t * poly
    poly = 0.5 * -0.284496736 + t * poly
    q = t * (0.5 * 0.254829592 + t * poly) * e
    phi = jnp.where(a >= 0.0, 1.0 - q, q)
    return a * phi, phi + (a * 0.3989422804014327) * e


def pipelined(n, product, use, bufs):
    a, b = bufs
    product(0, a)
    steps = (n - 1) // 2

    def body(i):
        g = 2 * i
        product(g + 1, b)
        use(g, a)
        product(g + 2, a)
        use(g + 1, b)

    loop(0, steps, body)
    if n % 2 == 0:
        product(n - 1, b)
        use(n - 2, a)
        use(n - 1, b)
    else:
        use(n - 1, a)


def store_product(buf, x, w):
    m, n = x.shape[0], w.shape[1]
    buf[8 : 8 + m, 0:n] = jnp.dot(x, w, preferred_element_type=F32)
    buf[8 + m : 16 + m, 0:n] = jnp.zeros((8, n), F32)


def both_halves(own, near, start, n):
    m, lanes = n * own.shape[1], own.shape[2]
    return jnp.concatenate(
        [own[pl.ds(start, n)].reshape(m, lanes), near[pl.ds(start, n)].reshape(m, lanes)], axis=1
    )


def taps(buf, start, size, n, at=0, width=None):
    width = n if width is None else width
    lo = 8 + start
    return (
        buf[lo : lo + size, n + at : n + at + width]
        + buf[lo - 1 : lo - 1 + size, at : at + width]
        + buf[lo + 1 : lo + 1 + size, 2 * n + at : 2 * n + at + width]
    )


def lane_taps(c):
    return pltpu.roll(c[0:8], 1, 1) + c[8:16] + pltpu.roll(c[16:24], 255, 1)


def nt(a, b):
    return lax.dot_general(a, b, (((1,), (1,)), ((), ())), preferred_element_type=F32)


def tn(a, b):
    return lax.dot_general(a, b, (((0,), (0,)), ((), ())), preferred_element_type=F32)


def loop(lo, hi, body):
    lax.fori_loop(lo, hi, lambda i, c: (body(i), c)[1], 0)


def color_column(values):
    c = iota((8, 1), 0) % 4
    out = jnp.zeros((8, 1), F32)
    for k, v in enumerate(values):
        out = jnp.where(c == k, v, out)
    return out


def stats_kernel(n, x_ref, o_ref):
    x_ref = x_ref.ready()
    rows, cols, channels = x_ref.shape

    def body(r, carry):
        s, q = carry
        for i in range(4):
            x = x_ref[4 * r + i].astype(F32).reshape(cols // 8, 8, channels)
            s = s + jnp.sum(x, axis=0)
            q = q + jnp.sum(x * x, axis=0)
        return s, q

    z = jnp.zeros((8, channels), F32)
    s, q = lax.fori_loop(0, rows // 4, body, (z, z))
    o_ref[...] = jnp.broadcast_to(group_rows(s, q), (n, 128))


def slab_kernel(x, up, down, right, left, sems):
    rows, cols, _ = x.shape
    h = HALO
    copies = []
    for out, at in ((right, cols - h), (left, 0)):
        for src, r in ((up, 0), (x, h), (down, h + rows)):
            k = len(copies)
            dst = out.at[pl.ds(r, src.shape[0])]
            copies.append(pltpu.make_async_copy(src.at[:, pl.ds(at, h)], dst, sems.at[k]))
            copies[-1].start()
    for c in copies:
        c.wait()


def forward_kernel(
    dims,
    idx,
    dbias,
    lat_hbm,
    up,
    down,
    left,
    right,
    stats,
    vecs,
    wd,
    w1,
    w2,
    w3,
    w4,
    gram,
    norm,
    o_slope1,
    o_feat2,
    o_slope2,
    o_slope3,
    o_feat4,
    o_slope4,
    o_sact,
    lat,
    tt,
    pixcol,
    y1,
    y1n,
    yp,
    ypn,
    pool,
    f3,
    fm,
    cm,
    hm,
    om,
    pa,
    pb,
    sems,
):
    rows, cols, image_rows, image_cols, count = dims
    h = HALO
    width = cols + 2 * h
    half = width // 2
    pairs = (rows + 2 * h) // 2
    pieces = (
        (lat_hbm, lat.at[pl.ds(h, rows), pl.ds(h, cols)]),
        (up, lat.at[pl.ds(0, h), pl.ds(h, cols)]),
        (down, lat.at[pl.ds(h + rows, h), pl.ds(h, cols)]),
        (left, lat.at[:, pl.ds(0, h)]),
        (right, lat.at[:, pl.ds(h + cols, h)]),
    )
    copies = [pltpu.make_async_copy(a, b, sems.at[i]) for i, (a, b) in enumerate(pieces)]
    for c in copies:
        c.start()
    slope1, feat2, slope2, slope3 = o_slope1.ref, o_feat2.ref, o_slope2.ref, o_slope3.ref
    feat4, slope4, sact = o_feat4.ref, o_slope4.ref, o_sact.ref

    pa[0:8] = jnp.zeros((8, pa.shape[1]), F32)
    pb[0:8] = jnp.zeros((8, pb.shape[1]), F32)
    tt[:, :, 128:256] = jnp.zeros((pairs, 72, 128), F32)
    pixcol[0] = jnp.zeros((32, 256), BF16)
    pixcol[pairs - 1] = jnp.zeros((32, 256), BF16)
    ypn[1, :, 64:128] = jnp.zeros((half, 64), BF16)
    ypn[pairs // 2 - 2, :, 0:64] = jnp.zeros((half, 64), BF16)

    row0 = idx[0] * rows - h
    col0 = idx[1] * cols - h

    def valid_rows(r):
        return jnp.where((row0 + r >= 0) & (row0 + r < image_rows), 1.0, 0.0).astype(F32)

    def valid_lanes(r):
        return jnp.full((1, 128), valid_rows(r), F32).astype(BF16)

    def col_mask(n, step, lanes):
        c = col0 + step * iota((n, lanes), 0)
        return jnp.where((c >= 0) & (c < image_cols), 1.0, 0.0).astype(BF16)

    cm[...] = col_mask(width, 1, 128)
    hm[...] = col_mask(half, 2, 128)
    own = iota((half, 128), 0)
    om[...] = jnp.where((own >= h // 2) & (own < h // 2 + cols // 2), 1.0, 0.0).astype(BF16)
    lane = iota((8, 256), 1)
    lmask = jnp.where((col0 + lane >= 0) & (col0 + lane < image_cols) & (lane < width), 1.0, 0.0)
    lmask = lmask.astype(F32)

    mean, rstd = norm_values(stats[...], count)
    norm[0:1] = mean
    norm[1:2] = rstd
    gain = vecs[0:1]
    scale = rstd * gain
    shift = vecs[1:2] - mean * scale
    b1, b2, b3, b4 = vecs[2:3], vecs[3:4], vecs[4:5], vecs[5:6]

    for c in copies:
        c.wait()
    wd = wd.ready()

    half_scale, half_shift = 0.5 * scale, 0.5 * shift

    def decode(p, own_rows):
        parts = []
        m = cm[...] * valid_lanes(2 * p)
        for i in range(2):
            t2 = lat[2 * p + i].astype(F32) * half_scale + half_shift
            th = jnp.tanh(t2)
            ts = t2 * th + t2
            parts.append(ts.astype(BF16) * m)
            if own_rows:
                th, t2 = th[h : h + cols], t2[h : h + cols]
                sl = (0.5 + 0.5 * th) * (1.0 + t2 * (1.0 - th))
                sact[2 * p + i - h] = (sl * gain).astype(BF16)
        tt[p, :, 0:width] = nt(wd[...], jnp.concatenate(parts, axis=1))

    def decode_two(p, own_rows):
        decode(p, own_rows)
        decode(p + 1, own_rows)

    loop(0, 4, lambda i: decode_two(2 * i, False))
    loop(4, 12, lambda i: decode_two(2 * i, True))
    loop(12, 16, lambda i: decode_two(2 * i, False))
    o_sact.send()
    w1, w2, w3, w4 = w1.ready(), w2.ready(), w3.ready(), w4.ready()

    pscale = color_column([0.5 / s for s in PIX_STD])
    pbias = color_column([((dbias[k] + 1.0) * 0.5 - PIX_MEAN[k]) * (1.0 / PIX_STD[k]) for k in range(3)])

    def pixels(p):
        c = tt[p, 0:24] + tt[p + 1, 24:48] + tt[p - 1, 48:72]
        x = (lane_taps(c) * pscale + pbias) * (lmask * valid_rows(2 * p))
        z = jnp.zeros((8, 256), F32)
        pixcol[p] = jnp.concatenate([pltpu.roll(x, 1, 1), x, pltpu.roll(x, 255, 1), z], axis=0).astype(BF16)

    def pixels_three(i):
        for k in range(3):
            pixels(1 + 3 * i + k)

    loop(0, (pairs - 2) // 3, pixels_three)

    def first_product(g, buf):
        for i in range(2):
            p = 1 + 2 * g + i
            lhs = pixcol[pl.ds(p - 1, 3), :, 0:width].reshape(96, width)
            buf[8 + i * width : 8 + (i + 1) * width, 0:128] = tn(lhs, w1[...])

    def first_use(g, buf):
        for i in range(2):
            p = 1 + 2 * g + i
            gl, sl = gelu_both(buf[8 + i * width : 8 + (i + 1) * width, 0:128] + b1)
            m = cm[...] * valid_lanes(2 * p)
            f = gl.astype(BF16) * m
            y1[p] = f
            y1n[p - 1, :, 0:64] = f[:, 0:64]
            y1n[p + 1, :, 64:128] = f[:, 64:128]
            slope1[p] = sl.astype(BF16) * m

    pipelined((pairs - 2) // 2, first_product, first_use, (pa, pb))
    o_slope1.send()

    pr = iota((half, width), 0)
    pc = iota((half, width), 1) // 2
    pool[...] = jnp.where(pr == pc, 0.25, 0.0).astype(BF16)

    def second_product(g, buf):
        store_product(buf, both_halves(y1, y1n, 2 + 4 * g, 4), w2[...])

    def second_use(g, buf):
        p0 = 2 + 4 * g
        for i in range(4):
            p = p0 + i
            f, sl = gelu_both(taps(buf, i * width, width, 128) + b2)
            m = cm[...] * valid_lanes(2 * p)
            fi = f.astype(BF16) * m
            feat2[p] = fi
            slope2[p] = sl.astype(BF16) * m
            half_sum = jnp.dot(pool[...], fi, preferred_element_type=F32)
            v = (half_sum + pltpu.roll(half_sum, 64, 1)).astype(BF16)
            k = 1 + 2 * g + i // 2
            if i % 2 == 0:
                yp[k, :, 0:64] = v[:, 0:64]
                ypn[k - 1, :, 0:64] = v[:, 0:64]
            else:
                yp[k, :, 64:128] = v[:, 64:128]
                ypn[k + 1, :, 64:128] = v[:, 64:128]

    pipelined(7, second_product, second_use, (pa, pb))
    o_feat2.send()
    o_slope2.send()

    def third_product(g, buf):
        store_product(buf, both_halves(yp, ypn, 1 + 2 * g, 2), w3[...])

    def wide_use(k0, buf, n, bias, keep):
        for i in range(n):
            m = hm[...] * valid_lanes(4 * (k0 + i))
            for q in range(2):
                f, sl = gelu_both(taps(buf, i * half, half, 256, q * 128, 128) + bias)
                keep(2 * (k0 + i) + q, f.astype(BF16) * m, sl.astype(BF16) * m)

    def third_keep(r, f, sl):
        f3[r] = f
        slope3[r] = sl

    pipelined(7, third_product, lambda g, buf: wide_use(1 + 2 * g, buf, 2, b3, third_keep), (pa, pb))
    o_slope3.send()

    def fourth_product(g, buf):
        lhs = []
        for i in range(4):
            r = 2 * (2 + 4 * g + i)
            lhs.append(jnp.concatenate([f3[r - 1], f3[r], f3[r + 1], f3[r + 2]], axis=1))
        store_product(buf, jnp.concatenate(lhs, axis=0), w4[...])

    def fourth_keep(r, f, sl):
        feat4[r] = f
        slope4[r] = sl
        fm[r] = f * om[...]

    pipelined(3, fourth_product, lambda g, buf: wide_use(2 + 4 * g, buf, 4, b4, fourth_keep), (pa, pb))
    o_feat4.send()
    o_slope4.send()

    a = fm[8:24].reshape(16 * half, 128)
    gram[0:128] = tn(a, a)
    b = feat2[8:24, h : h + cols, :].reshape(16 * cols, 128)
    gram[128:256] = tn(b, b)


def backward_kernel(
    dims,
    idx,
    totals,
    exlow,
    exhigh,
    slope1,
    feat2,
    slope2,
    slope3,
    feat4,
    slope4,
    sact,
    lat,
    norm,
    w4t,
    w3t,
    w2t,
    w1t,
    wdt,
    o_dxh,
    sums,
    loss,
    sw1,
    sw2,
    b4,
    b3,
    y2,
    y2n,
    spread,
    tt,
    brgb,
    pa,
    pb,
):
    rows, cols, image_rows, image_cols, _ = dims
    h = HALO
    width = cols + 2 * h
    half = width // 2
    npix = image_rows * image_cols
    row0 = idx[0] * rows - h
    col0 = idx[1] * cols - h

    def valid_rows(r):
        return jnp.where((row0 + r >= 0) & (row0 + r < image_rows), 1.0, 0.0).astype(F32)

    lane = iota((8, 256), 1)
    lmask = jnp.where((col0 + lane >= 0) & (col0 + lane < image_cols) & (lane < width), 1.0, 0.0)
    lmask = lmask.astype(F32)

    g1 = totals[128:256]
    g1 = g1 + pltpu.roll(pltpu.roll(g1, 64, 0), 64, 1)
    same = (iota((128, 128), 0) // 64) == (iota((128, 128), 1) // 64)
    gap1 = jnp.where(same, g1 * (1.0 / npix) - exlow[...], 0.0)
    gap2 = totals[0:128] * (4.0 / npix) - exhigh[...]
    value = jnp.sum(gap1 * gap1) * (0.5 / 4096.0) + jnp.sum(gap2 * gap2) * (1.0 / 16384.0)
    loss[...] = jnp.broadcast_to(value, loss.shape)
    for gap, sw in ((gap1, sw1), (gap2, sw2)):
        sym = 2.0 * (gap + gap.T)
        upper = sym.astype(BF16)
        sw[0:128] = upper
        sw[128:256] = (sym - upper.astype(F32)).astype(BF16)

    pa[0:8] = jnp.zeros((8, pa.shape[1]), F32)
    pb[0:8] = jnp.zeros((8, pb.shape[1]), F32)
    zrow = jnp.zeros((half, 128), BF16)
    b4[3] = zrow
    b4[28] = zrow
    tt[6] = jnp.zeros((72, 256), F32)
    tt[25] = jnp.zeros((72, 256), F32)
    tt[:, :, 128:256] = jnp.zeros((tt.shape[0], 72, 128), F32)

    def back4(g):
        r0 = 4 + 4 * g
        x = feat4[pl.ds(r0, 4)].reshape(4 * half, 128)
        y = jnp.dot(jnp.concatenate([x, x], axis=1), sw2[...], preferred_element_type=F32)
        y = y * slope4[pl.ds(r0, 4)].reshape(4 * half, 128).astype(F32)
        b4[pl.ds(r0, 4)] = y.astype(BF16).reshape(4, half, 128)

    feat4, slope4 = feat4.ready(), slope4.ready()
    loop(0, 6, back4)
    slope3, w4t, w3t = slope3.ready(), w4t.ready(), w3t.ready()

    def wide(k0, n, src, w, buf):
        lhs = []
        for i in range(n):
            r = 2 * (k0 + i)
            lhs.append(jnp.concatenate([src[r - 1], src[r], src[r + 1], src[r + 2]], axis=1))
        store_product(buf, jnp.concatenate(lhs, axis=0), w[...])

    def back3(g, buf):
        k0 = 2 + 4 * g
        for i in range(4):
            for q in range(2):
                r = 2 * (k0 + i) + q
                part = taps(buf, i * half, half, 256, q * 128, 128)
                b3[r] = (part * slope3[r].astype(F32)).astype(BF16)

    pipelined(3, lambda g, buf: wide(2 + 4 * g, 4, b4, w4t, buf), back3, (pa, pb))
    feat2, slope2 = feat2.ready(), slope2.ready()

    ur = iota((width, width), 0) // 2
    uc = iota((width, width), 1) % half
    spread[...] = jnp.where(ur == uc, 0.25, 0.0).astype(BF16)
    first_half = iota((width, 128), 1) < 64

    def back2(g, buf):
        k0 = 3 + 2 * g
        for i in range(2):
            gp = taps(buf, i * half, half, 128)
            upper = gp.astype(BF16)
            lower = (gp - upper.astype(F32)).astype(BF16)
            r = jnp.dot(spread[...], jnp.concatenate([upper, lower], axis=0), preferred_element_type=F32)
            rr = pltpu.roll(r, 64, 1)
            for q in range(2):
                p = 2 * (k0 + i) + q
                sp = jnp.where(first_half, r, rr) if q == 0 else jnp.where(first_half, rr, r)
                x = feat2[p]
                gt = jnp.dot(jnp.concatenate([x, x], axis=1), sw1[...], preferred_element_type=F32)
                b = ((sp + gt) * slope2[p].astype(F32)).astype(BF16)
                y2[p] = b
                y2n[p - 1, :, 0:64] = b[:, 0:64]
                y2n[p + 1, :, 64:128] = b[:, 64:128]

    pipelined(5, lambda g, buf: wide(3 + 2 * g, 2, b3, w3t, buf), back2, (pa, pb))
    slope1, w2t, w1t = slope1.ready(), w2t.ready(), w1t.ready()

    def back1_product(g, buf):
        store_product(buf, both_halves(y2, y2n, 7 + 3 * g, 3), w2t[...])

    def back1(g, buf):
        for i in range(3):
            p = 7 + 3 * g + i
            b = (taps(buf, i * width, width, 128) * slope1[p].astype(F32)).astype(BF16)
            tt[p, :, 0:width] = nt(w1t[...], b)

    pipelined(6, back1_product, back1, (pa, pb))

    pscale = color_column([0.5 / s for s in PIX_STD])

    def colors(p):
        c = tt[p, 0:24] + tt[p + 1, 24:48] + tt[p - 1, 48:72]
        x = lane_taps(c) * pscale * (lmask * valid_rows(2 * p))
        parts = [pltpu.roll(x, 256 - h + d, 1)[:, 0:cols] for d in (1, 0, -1)]
        z = jnp.zeros((8, cols), F32)
        brgb[p] = jnp.concatenate(parts + [z], axis=0).astype(BF16)

    def colors_three(i):
        for k in range(3):
            colors(7 + 3 * i + k)

    loop(0, 6, colors_three)

    mean, rstd = norm[0:1], norm[1:2]
    offset = mean * rstd
    sact, lat, wdt = sact.ready(), lat.ready(), wdt.ready()
    dxh = o_dxh.ref

    def last_two(i, carry):
        return last(9 + 2 * i, last(8 + 2 * i, carry))

    def last(p, carry):
        s, q = carry
        y = tn(brgb[pl.ds(p - 1, 3)].reshape(96, cols), wdt[...])
        for i in range(2):
            r = 2 * (p - 8) + i
            d = y[:, i * 128 : (i + 1) * 128] * sact[r].astype(F32)
            xh = lat[r].astype(F32) * rstd - offset
            dxh[r] = d.astype(BF16)
            s = s + jnp.sum(d.reshape(cols // 8, 8, 128), axis=0)
            q = q + jnp.sum((d * xh).reshape(cols // 8, 8, 128), axis=0)
        return s, q

    z = jnp.zeros((8, 128), F32)
    s, q = lax.fori_loop(0, 8, last_two, (z, z))
    o_dxh.send()
    sums[...] = jnp.broadcast_to(group_rows(s, q), sums.shape)


def final_kernel(count, lat, dxh, norm, sums, out_hbm, lbuf, dbuf, obuf, sems):
    rows = obuf.shape[0]
    parts = 4
    size = rows // parts
    arriving, leaving = [], []
    for k in range(parts):
        at = pl.ds(k * size, size)
        arriving.append(pltpu.make_async_copy(lat.at[at], lbuf.at[at], sems.at[k]))
        arriving.append(pltpu.make_async_copy(dxh.at[at], dbuf.at[at], sems.at[parts + k]))
        leaving.append(pltpu.make_async_copy(obuf.at[at], out_hbm.at[at], sems.at[2 * parts + k]))
    for c in arriving:
        c.start()
    mean, rstd = norm[0:1], norm[1:2]
    n1, n2 = group_values(sums[...], count)
    b = rstd * rstd * n2
    c = rstd * n1 - b * mean

    def row(r):
        obuf[r] = (dbuf[r].astype(F32) * rstd - lbuf[r].astype(F32) * b - c).astype(BF16)

    for k in range(parts):
        arriving[2 * k].wait()
        arriving[2 * k + 1].wait()
        loop(k * size // 2, (k + 1) * size // 2, lambda i: (row(2 * i), row(2 * i + 1)))
        leaving[k].start()
    for x in leaving:
        x.wait()


def placed_at(x, space):
    return x if INTERPRET else pltpu.with_memory_space_constraint(x, space)


class Arriving:
    def __init__(self, src, dst, sem):
        self.dst = dst
        self.copy = pltpu.make_async_copy(src, dst, sem)
        self.copy.start()

    def ready(self):
        self.copy.wait()
        return self.dst


class Leaving:
    def __init__(self, src, dst, sem):
        self.ref = src
        self.copy = pltpu.make_async_copy(src, dst, sem)

    def send(self):
        self.copy.start()


def call(kernel, outs, scratch, args, kinds, out_kinds):
    spaces = {"s": pltpu.SMEM, "a": pl.ANY,  "d": pl.ANY, "v": pltpu.VMEM, "m": pltpu.VMEM}
    late_in = [i for i, k in enumerate(kinds) if k == "d"]
    late_out = [i for i, k in enumerate(out_kinds) if k == "d"]
    buffers = [pltpu.VMEM(args[i].shape, args[i].dtype) for i in late_in]
    buffers += [pltpu.VMEM(*outs[i]) for i in late_out]
    sems = [pltpu.SemaphoreType.DMA((len(buffers),))] if buffers else []

    def body(*refs):
        refs = list(refs)
        n_in, n_out = len(args), len(outs)
        ins, results, rest = refs[:n_in], refs[n_in : n_in + n_out], refs[n_in + n_out :]
        own, extra = rest[: len(scratch)], rest[len(scratch) :]
        leaving = []
        for j, i in enumerate(late_in):
            ins[i] = Arriving(ins[i], extra[j], extra[-1].at[j])
        for j, i in enumerate(late_out):
            k = len(late_in) + j
            results[i] = Leaving(extra[k], results[i], extra[-1].at[k])
            leaving.append(results[i])
        kernel(*ins, *results, *own)
        for x in leaving:
            x.copy.wait()

    return pl.pallas_call(
        body,
        out_shape=[jax.ShapeDtypeStruct(s, d) if INTERPRET else pltpu.HBM(s, d) for s, d in outs],
        in_specs=[pl.BlockSpec(memory_space=spaces[k]) for k in kinds],
        out_specs=[pl.BlockSpec(memory_space=spaces[k]) for k in out_kinds],
        scratch_shapes=list(scratch) + buffers + sems,
        compiler_params=pltpu.CompilerParams(vmem_limit_bytes=VMEM_LIMIT),
        interpret=INTERPRET,
    )(*[a if k == "s" else placed_at(a, pltpu.VMEM if k == "m" else pltpu.HBM) for a, k in zip(args, kinds)])


def local(
    latent,
    gain,
    bias,
    decoder_weight,
    decoder_bias,
    first_weight,
    first_bias,
    second_weight,
    second_bias,
    third_weight,
    third_bias,
    fourth_weight,
    fourth_bias,
    exemplar_low,
    exemplar_high,
):
    rows, cols, channels = latent.shape
    nrow, ncol = lax.axis_size("row"), lax.axis_size("col")
    n = nrow * ncol
    both = ("row", "col")
    h = HALO
    width = cols + 2 * h
    half = width // 2
    pairs = (rows + 2 * h) // 2
    image_rows, image_cols = rows * nrow, cols * ncol
    count = image_rows * image_cols * (channels // GROUPS)
    dims = (rows, cols, image_rows, image_cols, count)

    def shifted(x, axis, step):
        size = lax.axis_size(axis)
        return lax.ppermute(x, axis, [(i, i + step) for i in range(size) if 0 <= i + step < size])

    def everyone(x):
        return lax.all_to_all(x, both, 0, 0, tiled=True)

    up = shifted(latent[rows - h :], "row", 1)
    down = shifted(latent[:h], "row", -1)
    (mine,) = call(lambda *r: stats_kernel(n, *r), [((n, 128), F32)], [], [latent], "d", "v")
    stats = everyone(mine)
    right_edge, left_edge = call(
        slab_kernel,
        [((2 * pairs, h, 128), BF16)] * 2,
        [pltpu.SemaphoreType.DMA((6,))],
        [latent, up, down],
        "aaa",
        "aa",
    )
    left = shifted(right_edge, "col", 1)
    right = shifted(left_edge, "col", -1)

    idx = jnp.stack([lax.axis_index("row"), lax.axis_index("col"), jnp.int32(0)]).astype(jnp.int32)
    vecs = jnp.concatenate(
        [
            gain,
            bias,
            first_bias,
            first_bias,
            second_bias,
            second_bias,
            third_bias,
            fourth_bias,
            jnp.zeros((256,), F32),
        ]
    ).reshape(8, 128)
    dec = jnp.pad(jnp.transpose(decoder_weight, (0, 1, 3, 2)), ((0, 0), (0, 0), (0, 1), (0, 0)))
    fst = jnp.pad(first_weight, ((0, 0), (0, 0), (0, 1), (0, 0)))
    wd, w1, w2, w3, w4, w4t, w3t, w2t, w1t, wdt = call(
        weights_kernel,
        [
            ((72, 256), BF16),
            ((96, 128), BF16),
            ((256, 384), BF16),
            ((256, 768), BF16),
            ((512, 768), BF16),
            ((512, 768), BF16),
            ((512, 384), BF16),
            ((256, 384), BF16),
            ((72, 128), BF16),
            ((96, 256), BF16),
        ],
        [],
        [
            dec.reshape(36, 128),
            fst.reshape(36, 64),
            second_weight,
            third_weight,
            fourth_weight,
            *narrow_tables(),
        ],
        "v" * 7,
        "v" * 10,
    )

    states = call(
        lambda *r: forward_kernel(dims, *r),
        [
            ((256, 128), F32),
            ((8, 128), F32),
            ((pairs, width, 128), BF16),
            ((pairs, width, 128), BF16),
            ((pairs, width, 128), BF16),
            ((pairs, half, 128), BF16),
            ((pairs, half, 128), BF16),
            ((pairs, half, 128), BF16),
            ((rows, cols, 128), BF16),
        ],
        [
            pltpu.VMEM((2 * pairs, width, 128), BF16),
            pltpu.VMEM((pairs, 72, 256), F32),
            pltpu.VMEM((pairs, 32, 256), BF16),
            pltpu.VMEM((pairs, width, 128), BF16),
            pltpu.VMEM((pairs, width, 128), BF16),
            pltpu.VMEM((pairs // 2, half, 128), BF16),
            pltpu.VMEM((pairs // 2, half, 128), BF16),
            pltpu.VMEM((half, width), BF16),
            pltpu.VMEM((pairs, half, 128), BF16),
            pltpu.VMEM((pairs, half, 128), BF16),
            pltpu.VMEM((width, 128), BF16),
            pltpu.VMEM((half, 128), BF16),
            pltpu.VMEM((half, 128), BF16),
            pltpu.VMEM((4 * width + 16, 768), F32),
            pltpu.VMEM((4 * width + 16, 768), F32),
            pltpu.SemaphoreType.DMA((5,)),
        ],
        [idx, decoder_bias, latent, up, down, left, right, stats, vecs, wd, w1, w2, w3, w4],
        "ssaaammmv" + "d" * 5,
        "vv" + "d" * 7,
    )
    gram, norm = states[:2]
    mine = everyone(gram).reshape(n, 256 // n, 128).sum(axis=0)
    totals = everyone(jnp.broadcast_to(mine[None], (n, 256 // n, 128)).reshape(256, 128))
    exlow = jnp.tile(exemplar_low, (2, 2))

    dxh, sums, loss = call(
        lambda *r: backward_kernel(dims, *r),
        [((rows, cols, 128), BF16), ((n, 128), F32), ((8, 128), F32)],
        [
            pltpu.VMEM((256, 128), BF16),
            pltpu.VMEM((256, 128), BF16),
            pltpu.VMEM((pairs, half, 128), BF16),
            pltpu.VMEM((pairs, half, 128), BF16),
            pltpu.VMEM((pairs, width, 128), BF16),
            pltpu.VMEM((pairs, width, 128), BF16),
            pltpu.VMEM((width, width), BF16),
            pltpu.VMEM((pairs, 72, 256), F32),
            pltpu.VMEM((pairs, 32, cols), BF16),
            pltpu.VMEM((4 * width + 16, 768), F32),
            pltpu.VMEM((4 * width + 16, 768), F32),
        ],
        [idx, totals, exlow, exemplar_high, *states[2:], latent, norm, w4t, w3t, w2t, w1t, wdt],
        "smvv" + "d" * 8 + "v" + "d" * 5,
        "dvv",
    )
    sums = everyone(sums)

    tile = (rows, cols, channels)
    (out,) = call(
        lambda *r: final_kernel(count, *r),
        [(tile, BF16)],
        [pltpu.VMEM(tile, BF16)] * 3 + [pltpu.SemaphoreType.DMA((12,))],
        [latent, dxh, norm, sums],
        "aavm",
        "a",
    )
    return out, loss[0, 0]


def solution(mesh):
    placed = (P("row", "col", None),) + (P(),) * 14
    return jax.shard_map(
        local, mesh=mesh, in_specs=placed, out_specs=(P("row", "col", None), P()), check_vma=False
    )
```

```python
import jax
import jax.numpy as jnp
import numpy as np
from jax import lax
from jax.experimental import pallas as pl
from jax.experimental.pallas import tpu as pltpu
from jax.sharding import PartitionSpec as P

GROUPS = 32
EPS = 1e-05
PIX_MEAN = (0.485, 0.456, 0.406)
PIX_STD = (0.229, 0.224, 0.225)
HALO = 16
F32 = jnp.float32
BF16 = jnp.bfloat16
INTERPRET = False
VMEM_LIMIT = 40 * 1024 * 1024


def narrow_tables():
    out_fwd = np.zeros((2, 3, 3, 2, 4, 3, 3, 4), np.float32)
    out_bwd = np.zeros_like(out_fwd)
    in_fwd = np.zeros((2, 3, 3, 2, 4, 3, 3, 4), np.float32)
    in_bwd = np.zeros_like(in_fwd)
    for k, s in enumerate((0, -1, 1)):
        for dx in range(3):
            for q in range(2):
                for i in range(2):
                    dy = i - q - 2 * s + 1
                    if 0 <= dy < 3:
                        for c in range(3):
                            out_fwd[i, k, dx, q, c, dy, dx, c] = 1
                            out_bwd[i, k, dx, q, c, 2 - dy, 2 - dx, c] = 1
    for k, s in enumerate((-1, 0, 1)):
        for dx in range(3):
            for q in range(2):
                for i in range(2):
                    dy = 2 * s + i - q + 1
                    if 0 <= dy < 3:
                        for c in range(3):
                            in_fwd[q, k, dx, i, c, dy, dx, c] = 1
                            in_bwd[q, k, dx, i, c, 2 - dy, 2 - dx, c] = 1
    outs = np.concatenate([out_fwd.reshape(2, 72, 36), out_bwd.reshape(2, 72, 36)], 0)
    ins = np.concatenate([in_fwd.reshape(2, 3, 24, 36), in_bwd.reshape(2, 3, 24, 36)], 0)
    ins = np.pad(ins, ((0, 0), (0, 0), (0, 8), (0, 0))).reshape(4, 96, 36)
    return jnp.asarray(outs, BF16), jnp.asarray(ins, BF16)


def place(t, x):
    return jnp.dot(t, x, preferred_element_type=F32)


def tap(w, dy, dx):
    return w[dy, dx] if 0 <= dy < 3 else jnp.zeros(w.shape[2:], BF16)


def forward_weights(dec, fst, w2r, w3r, w4r, outs, ins, wd, w1, w2, w3, w4):
    d, f = dec[...], fst[...]
    for i in range(2):
        wd[:, i * 128 : (i + 1) * 128] = place(outs[i], d).astype(BF16)
    w1[...] = jnp.concatenate([place(ins[0], f), place(ins[1], f)], axis=1).astype(BF16)
    for k, j in enumerate((1, 2, 3, 0)):
        for dx in range(3):
            pair = [tap(w2r, j - q, dx) for q in range(2)]
            w2[k * 64 : (k + 1) * 64, dx * 128 : (dx + 1) * 128] = jnp.concatenate(pair, axis=1)
            for q in range(2):
                at = dx * 256 + q * 128
                w3[k * 64 : (k + 1) * 64, at : at + 128] = tap(w3r, j - q, dx)
    for j in range(4):
        for dx in range(3):
            for q in range(2):
                at = dx * 256 + q * 128
                w4[j * 128 : (j + 1) * 128, at : at + 128] = tap(w4r, j - q, dx)


def backward_weights(dec, fst, w2r, w3r, w4r, outs, ins, w4t, w3t, w2t, w1t, wdt):
    d, f = dec[...], fst[...]
    for i in range(2):
        wdt[:, i * 128 : (i + 1) * 128] = place(ins[2 + i], d).astype(BF16)
    w1t[...] = jnp.concatenate([place(outs[2], f), place(outs[3], f)], axis=1).astype(BF16)
    for k, j in enumerate((1, 2, 3, 0)):
        for dx in range(3):
            pair = [tap(w2r, 2 - j + q, 2 - dx) for q in range(2)]
            w2t[k * 64 : (k + 1) * 64, dx * 128 : (dx + 1) * 128] = jnp.concatenate(pair, axis=0).T
    for j in range(4):
        for dx in range(3):
            pair = [tap(w3r, 2 - j + q, 2 - dx) for q in range(2)]
            w3t[j * 128 : (j + 1) * 128, dx * 128 : (dx + 1) * 128] = jnp.concatenate(pair, axis=0).T
            for q in range(2):
                at = dx * 256 + q * 128
                w4t[j * 128 : (j + 1) * 128, at : at + 128] = tap(w4r, 2 - j + q, 2 - dx).T


def iota(shape, axis):
    return lax.broadcasted_iota(jnp.int32, shape, axis)


def split3(x):
    hi = x.astype(BF16).astype(F32)
    mid = (x - hi).astype(BF16).astype(F32)
    lo = x - hi - mid
    r = iota((16, 128), 0)
    return jnp.where(r == 0, hi, jnp.where(r == 1, mid, jnp.where(r == 2, lo, 0.0))).astype(BF16)


def exact_dot(x, table):
    return jnp.sum(jnp.dot(split3(x), table, preferred_element_type=F32), axis=0, keepdims=True)


def group_rows(s, q):
    c = iota((128, 128), 0) // (128 // GROUPS)
    l = iota((128, 128), 1)
    g1 = jnp.where(l == c, 1.0, 0.0).astype(BF16)
    g2 = jnp.where(l == c + GROUPS, 1.0, 0.0).astype(BF16)
    s = jnp.sum(s, axis=0, keepdims=True)
    q = jnp.sum(q, axis=0, keepdims=True)
    return exact_dot(s, g1) + exact_dot(q, g2)


def group_values(rows, count):
    tot = jnp.sum(rows, axis=0, keepdims=True)
    l = iota((128, 256), 0)
    c = iota((128, 256), 1)
    want = (c % 128) // (128 // GROUPS) + GROUPS * (c // 128)
    e = jnp.where(l == want, 1.0, 0.0).astype(BF16)
    v = exact_dot(tot, e) * (1.0 / count)
    return v[:, 0:128], v[:, 128:256]


def norm_values(rows, count):
    mean, msq = group_values(rows, count)
    return mean, lax.rsqrt(msq - mean * mean + EPS)


def gelu_both(a):
    e = jnp.exp2(a * a * (-0.5 * 1.4426950408889634))
    t = 1.0 / (1.0 + jnp.abs(a) * (0.3275911 * 0.7071067811865476))
    poly = 0.5 * -1.453152027 + t * (0.5 * 1.061405429)
    poly = 0.5 * 1.421413741 + t * poly
    poly = 0.5 * -0.284496736 + t * poly
    q = t * (0.5 * 0.254829592 + t * poly) * e
    phi = jnp.where(a >= 0.0, 1.0 - q, q)
    return a * phi, phi + (a * 0.3989422804014327) * e


def pipelined(n, product, use, bufs):
    a, b = bufs
    product(0, a)
    steps = (n - 1) // 2

    def body(i):
        g = 2 * i
        product(g + 1, b)
        use(g, a)
        product(g + 2, a)
        use(g + 1, b)

    loop(0, steps, body)
    if n % 2 == 0:
        product(n - 1, b)
        use(n - 2, a)
        use(n - 1, b)
    else:
        use(n - 1, a)


def store_product(buf, x, w):
    m, n = x.shape[0], w.shape[1]
    buf[8 : 8 + m, 0:n] = jnp.dot(x, w, preferred_element_type=F32)
    buf[8 + m : 16 + m, 0:n] = jnp.zeros((8, n), F32)


def both_halves(own, near, start, n):
    m, lanes = n * own.shape[1], own.shape[2]
    return jnp.concatenate(
        [own[pl.ds(start, n)].reshape(m, lanes), near[pl.ds(start, n)].reshape(m, lanes)], axis=1
    )


def taps(buf, start, size, n, at=0, width=None):
    width = n if width is None else width
    lo = 8 + start
    return (
        buf[lo : lo + size, n + at : n + at + width]
        + buf[lo - 1 : lo - 1 + size, at : at + width]
        + buf[lo + 1 : lo + 1 + size, 2 * n + at : 2 * n + at + width]
    )


def lane_taps(c):
    return pltpu.roll(c[0:8], 1, 1) + c[8:16] + pltpu.roll(c[16:24], 255, 1)


def nt(a, b):
    return lax.dot_general(a, b, (((1,), (1,)), ((), ())), preferred_element_type=F32)


def tn(a, b):
    return lax.dot_general(a, b, (((0,), (0,)), ((), ())), preferred_element_type=F32)


def loop(lo, hi, body):
    lax.fori_loop(lo, hi, lambda i, c: (body(i), c)[1], 0)


def color_column(values):
    c = iota((8, 1), 0) % 4
    out = jnp.zeros((8, 1), F32)
    for k, v in enumerate(values):
        out = jnp.where(c == k, v, out)
    return out


def stats_kernel(n, x_ref, o_ref):
    x_ref = x_ref.ready()
    rows, cols, channels = x_ref.shape

    def body(r, carry):
        s, q = carry
        for i in range(4):
            x = x_ref[4 * r + i].astype(F32).reshape(cols // 8, 8, channels)
            s = s + jnp.sum(x, axis=0)
            q = q + jnp.sum(x * x, axis=0)
        return s, q

    z = jnp.zeros((8, channels), F32)
    s, q = lax.fori_loop(0, rows // 4, body, (z, z))
    o_ref[...] = jnp.broadcast_to(group_rows(s, q), (n, 128))


def slab_kernel(x, up, down, right, left):
    rows, cols, _ = x.shape
    h = HALO
    for out, at in ((right, cols - h), (left, 0)):
        for src, r in ((up, 0), (x, h), (down, h + rows)):
            out[r : r + src.shape[0]] = src[:, at : at + h]


def forward_kernel(
    dims,
    idx,
    dbias,
    lat_hbm,
    up,
    down,
    left,
    right,
    stats,
    vecs,
    wd,
    w1,
    w2,
    w3,
    w4,
    gram,
    norm,
    o_slope1,
    o_feat2,
    o_slope2,
    o_slope3,
    o_feat4,
    o_slope4,
    o_sact,
    lat,
    tt,
    pixcol,
    y1,
    y1n,
    yp,
    ypn,
    pool,
    f3,
    fm,
    cm,
    hm,
    om,
    pa,
    pb,
    sems,
):
    rows, cols, image_rows, image_cols, count = dims
    h = HALO
    width = cols + 2 * h
    half = width // 2
    pairs = (rows + 2 * h) // 2
    pieces = (
        (lat_hbm, lat.at[pl.ds(h, rows), pl.ds(h, cols)]),
        (up, lat.at[pl.ds(0, h), pl.ds(h, cols)]),
        (down, lat.at[pl.ds(h + rows, h), pl.ds(h, cols)]),
        (left, lat.at[:, pl.ds(0, h)]),
        (right, lat.at[:, pl.ds(h + cols, h)]),
    )
    copies = [pltpu.make_async_copy(a, b, sems.at[i]) for i, (a, b) in enumerate(pieces)]
    for c in copies:
        c.start()
    slope1, feat2, slope2, slope3 = o_slope1.ref, o_feat2.ref, o_slope2.ref, o_slope3.ref
    feat4, slope4, sact = o_feat4.ref, o_slope4.ref, o_sact.ref

    pa[0:8] = jnp.zeros((8, pa.shape[1]), F32)
    pb[0:8] = jnp.zeros((8, pb.shape[1]), F32)
    tt[:, :, 128:256] = jnp.zeros((pairs, 72, 128), F32)
    pixcol[0] = jnp.zeros((32, 256), BF16)
    pixcol[pairs - 1] = jnp.zeros((32, 256), BF16)
    ypn[1, :, 64:128] = jnp.zeros((half, 64), BF16)
    ypn[pairs // 2 - 2, :, 0:64] = jnp.zeros((half, 64), BF16)

    row0 = idx[0] * rows - h
    col0 = idx[1] * cols - h

    def valid_rows(r):
        return jnp.where((row0 + r >= 0) & (row0 + r < image_rows), 1.0, 0.0).astype(F32)

    def valid_lanes(r):
        return jnp.full((1, 128), valid_rows(r), F32).astype(BF16)

    def col_mask(n, step, lanes):
        c = col0 + step * iota((n, lanes), 0)
        return jnp.where((c >= 0) & (c < image_cols), 1.0, 0.0).astype(BF16)

    cm[...] = col_mask(width, 1, 128)
    hm[...] = col_mask(half, 2, 128)
    own = iota((half, 128), 0)
    om[...] = jnp.where((own >= h // 2) & (own < h // 2 + cols // 2), 1.0, 0.0).astype(BF16)
    lane = iota((8, 256), 1)
    lmask = jnp.where((col0 + lane >= 0) & (col0 + lane < image_cols) & (lane < width), 1.0, 0.0)
    lmask = lmask.astype(F32)

    mean, rstd = norm_values(stats[...], count)
    norm[0:1] = mean
    norm[1:2] = rstd
    gain = vecs[0:1]
    scale = rstd * gain
    shift = vecs[1:2] - mean * scale
    b1, b2, b3, b4 = vecs[2:3], vecs[3:4], vecs[4:5], vecs[5:6]

    for c in copies:
        c.wait()
    wd = wd.ready()

    half_scale, half_shift = 0.5 * scale, 0.5 * shift

    def decode(p, own_rows):
        parts = []
        m = cm[...] * valid_lanes(2 * p)
        for i in range(2):
            t2 = lat[2 * p + i].astype(F32) * half_scale + half_shift
            th = jnp.tanh(t2)
            ts = t2 * th + t2
            parts.append(ts.astype(BF16) * m)
            if own_rows:
                th, t2 = th[h : h + cols], t2[h : h + cols]
                sl = (0.5 + 0.5 * th) * (1.0 + t2 * (1.0 - th))
                sact[2 * p + i - h] = (sl * gain).astype(BF16)
        tt[p, :, 0:width] = nt(wd[...], jnp.concatenate(parts, axis=1))

    def decode_two(p, own_rows):
        decode(p, own_rows)
        decode(p + 1, own_rows)

    loop(0, 4, lambda i: decode_two(2 * i, False))
    loop(4, 12, lambda i: decode_two(2 * i, True))
    loop(12, 16, lambda i: decode_two(2 * i, False))
    o_sact.send()
    w1, w2, w3, w4 = w1.ready(), w2.ready(), w3.ready(), w4.ready()

    pscale = color_column([0.5 / s for s in PIX_STD])
    pbias = color_column([((dbias[k] + 1.0) * 0.5 - PIX_MEAN[k]) * (1.0 / PIX_STD[k]) for k in range(3)])

    def pixels(p):
        c = tt[p, 0:24] + tt[p + 1, 24:48] + tt[p - 1, 48:72]
        x = (lane_taps(c) * pscale + pbias) * (lmask * valid_rows(2 * p))
        z = jnp.zeros((8, 256), F32)
        pixcol[p] = jnp.concatenate([pltpu.roll(x, 1, 1), x, pltpu.roll(x, 255, 1), z], axis=0).astype(BF16)

    def pixels_three(i):
        for k in range(3):
            pixels(1 + 3 * i + k)

    loop(0, (pairs - 2) // 3, pixels_three)

    def first_product(g, buf):
        for i in range(2):
            p = 1 + 2 * g + i
            lhs = pixcol[pl.ds(p - 1, 3), :, 0:width].reshape(96, width)
            buf[8 + i * width : 8 + (i + 1) * width, 0:128] = tn(lhs, w1[...])

    def first_use(g, buf):
        for i in range(2):
            p = 1 + 2 * g + i
            gl, sl = gelu_both(buf[8 + i * width : 8 + (i + 1) * width, 0:128] + b1)
            m = cm[...] * valid_lanes(2 * p)
            f = gl.astype(BF16) * m
            y1[p] = f
            y1n[p - 1, :, 0:64] = f[:, 0:64]
            y1n[p + 1, :, 64:128] = f[:, 64:128]
            slope1[p] = sl.astype(BF16) * m

    pipelined((pairs - 2) // 2, first_product, first_use, (pa, pb))
    o_slope1.send()

    pr = iota((half, width), 0)
    pc = iota((half, width), 1) // 2
    pool[...] = jnp.where(pr == pc, 0.25, 0.0).astype(BF16)

    def second_product(g, buf):
        store_product(buf, both_halves(y1, y1n, 2 + 4 * g, 4), w2[...])

    def second_use(g, buf):
        p0 = 2 + 4 * g
        for i in range(4):
            p = p0 + i
            f, sl = gelu_both(taps(buf, i * width, width, 128) + b2)
            m = cm[...] * valid_lanes(2 * p)
            fi = f.astype(BF16) * m
            feat2[p] = fi
            slope2[p] = sl.astype(BF16) * m
            half_sum = jnp.dot(pool[...], fi, preferred_element_type=F32)
            v = (half_sum + pltpu.roll(half_sum, 64, 1)).astype(BF16)
            k = 1 + 2 * g + i // 2
            if i % 2 == 0:
                yp[k, :, 0:64] = v[:, 0:64]
                ypn[k - 1, :, 0:64] = v[:, 0:64]
            else:
                yp[k, :, 64:128] = v[:, 64:128]
                ypn[k + 1, :, 64:128] = v[:, 64:128]

    pipelined(7, second_product, second_use, (pa, pb))
    o_feat2.send()
    o_slope2.send()

    def third_product(g, buf):
        store_product(buf, both_halves(yp, ypn, 1 + 2 * g, 2), w3[...])

    def wide_use(k0, buf, n, bias, keep):
        for i in range(n):
            m = hm[...] * valid_lanes(4 * (k0 + i))
            for q in range(2):
                f, sl = gelu_both(taps(buf, i * half, half, 256, q * 128, 128) + bias)
                keep(2 * (k0 + i) + q, f.astype(BF16) * m, sl.astype(BF16) * m)

    def third_keep(r, f, sl):
        f3[r] = f
        slope3[r] = sl

    pipelined(7, third_product, lambda g, buf: wide_use(1 + 2 * g, buf, 2, b3, third_keep), (pa, pb))
    o_slope3.send()

    def fourth_product(g, buf):
        lhs = []
        for i in range(4):
            r = 2 * (2 + 4 * g + i)
            lhs.append(jnp.concatenate([f3[r - 1], f3[r], f3[r + 1], f3[r + 2]], axis=1))
        store_product(buf, jnp.concatenate(lhs, axis=0), w4[...])

    def fourth_keep(r, f, sl):
        feat4[r] = f
        slope4[r] = sl
        fm[r] = f * om[...]

    pipelined(3, fourth_product, lambda g, buf: wide_use(2 + 4 * g, buf, 4, b4, fourth_keep), (pa, pb))
    o_feat4.send()
    o_slope4.send()

    a = fm[8:24].reshape(16 * half, 128)
    gram[0:128] = tn(a, a)
    b = feat2[8:24, h : h + cols, :].reshape(16 * cols, 128)
    gram[128:256] = tn(b, b)


def backward_kernel(
    dims,
    idx,
    totals,
    exlow,
    exhigh,
    slope1,
    feat2,
    slope2,
    slope3,
    feat4,
    slope4,
    sact,
    lat,
    norm,
    w4t,
    w3t,
    w2t,
    w1t,
    wdt,
    o_dxh,
    sums,
    loss,
    sw1,
    sw2,
    b4,
    b3,
    y2,
    y2n,
    spread,
    tt,
    brgb,
    pa,
    pb,
):
    rows, cols, image_rows, image_cols, _ = dims
    h = HALO
    width = cols + 2 * h
    half = width // 2
    npix = image_rows * image_cols
    row0 = idx[0] * rows - h
    col0 = idx[1] * cols - h

    def valid_rows(r):
        return jnp.where((row0 + r >= 0) & (row0 + r < image_rows), 1.0, 0.0).astype(F32)

    lane = iota((8, 256), 1)
    lmask = jnp.where((col0 + lane >= 0) & (col0 + lane < image_cols) & (lane < width), 1.0, 0.0)
    lmask = lmask.astype(F32)

    g1 = totals[128:256]
    g1 = g1 + pltpu.roll(pltpu.roll(g1, 64, 0), 64, 1)
    same = (iota((128, 128), 0) // 64) == (iota((128, 128), 1) // 64)
    gap1 = jnp.where(same, g1 * (1.0 / npix) - exlow[...], 0.0)
    gap2 = totals[0:128] * (4.0 / npix) - exhigh[...]
    value = jnp.sum(gap1 * gap1) * (0.5 / 4096.0) + jnp.sum(gap2 * gap2) * (1.0 / 16384.0)
    loss[...] = jnp.broadcast_to(value, loss.shape)
    for gap, sw in ((gap1, sw1), (gap2, sw2)):
        sym = 2.0 * (gap + gap.T)
        upper = sym.astype(BF16)
        sw[0:128] = upper
        sw[128:256] = (sym - upper.astype(F32)).astype(BF16)

    pa[0:8] = jnp.zeros((8, pa.shape[1]), F32)
    pb[0:8] = jnp.zeros((8, pb.shape[1]), F32)
    zrow = jnp.zeros((half, 128), BF16)
    b4[3] = zrow
    b4[28] = zrow
    tt[6] = jnp.zeros((72, 256), F32)
    tt[25] = jnp.zeros((72, 256), F32)
    tt[:, :, 128:256] = jnp.zeros((tt.shape[0], 72, 128), F32)

    def back4(g):
        r0 = 4 + 4 * g
        x = feat4[pl.ds(r0, 4)].reshape(4 * half, 128)
        y = jnp.dot(jnp.concatenate([x, x], axis=1), sw2[...], preferred_element_type=F32)
        y = y * slope4[pl.ds(r0, 4)].reshape(4 * half, 128).astype(F32)
        b4[pl.ds(r0, 4)] = y.astype(BF16).reshape(4, half, 128)

    feat4, slope4 = feat4.ready(), slope4.ready()
    loop(0, 6, back4)
    slope3, w4t, w3t = slope3.ready(), w4t.ready(), w3t.ready()

    def wide(k0, n, src, w, buf):
        lhs = []
        for i in range(n):
            r = 2 * (k0 + i)
            lhs.append(jnp.concatenate([src[r - 1], src[r], src[r + 1], src[r + 2]], axis=1))
        store_product(buf, jnp.concatenate(lhs, axis=0), w[...])

    def back3(g, buf):
        k0 = 2 + 4 * g
        for i in range(4):
            for q in range(2):
                r = 2 * (k0 + i) + q
                part = taps(buf, i * half, half, 256, q * 128, 128)
                b3[r] = (part * slope3[r].astype(F32)).astype(BF16)

    pipelined(3, lambda g, buf: wide(2 + 4 * g, 4, b4, w4t, buf), back3, (pa, pb))
    feat2, slope2 = feat2.ready(), slope2.ready()

    ur = iota((width, width), 0) // 2
    uc = iota((width, width), 1) % half
    spread[...] = jnp.where(ur == uc, 0.25, 0.0).astype(BF16)
    first_half = iota((width, 128), 1) < 64

    def back2(g, buf):
        k0 = 3 + 2 * g
        for i in range(2):
            gp = taps(buf, i * half, half, 128)
            upper = gp.astype(BF16)
            lower = (gp - upper.astype(F32)).astype(BF16)
            r = jnp.dot(spread[...], jnp.concatenate([upper, lower], axis=0), preferred_element_type=F32)
            rr = pltpu.roll(r, 64, 1)
            for q in range(2):
                p = 2 * (k0 + i) + q
                sp = jnp.where(first_half, r, rr) if q == 0 else jnp.where(first_half, rr, r)
                x = feat2[p]
                gt = jnp.dot(jnp.concatenate([x, x], axis=1), sw1[...], preferred_element_type=F32)
                b = ((sp + gt) * slope2[p].astype(F32)).astype(BF16)
                y2[p] = b
                y2n[p - 1, :, 0:64] = b[:, 0:64]
                y2n[p + 1, :, 64:128] = b[:, 64:128]

    pipelined(5, lambda g, buf: wide(3 + 2 * g, 2, b3, w3t, buf), back2, (pa, pb))
    slope1, w2t, w1t = slope1.ready(), w2t.ready(), w1t.ready()

    def back1_product(g, buf):
        store_product(buf, both_halves(y2, y2n, 7 + 3 * g, 3), w2t[...])

    def back1(g, buf):
        for i in range(3):
            p = 7 + 3 * g + i
            b = (taps(buf, i * width, width, 128) * slope1[p].astype(F32)).astype(BF16)
            tt[p, :, 0:width] = nt(w1t[...], b)

    pipelined(6, back1_product, back1, (pa, pb))

    pscale = color_column([0.5 / s for s in PIX_STD])

    def colors(p):
        c = tt[p, 0:24] + tt[p + 1, 24:48] + tt[p - 1, 48:72]
        x = lane_taps(c) * pscale * (lmask * valid_rows(2 * p))
        parts = [pltpu.roll(x, 256 - h + d, 1)[:, 0:cols] for d in (1, 0, -1)]
        z = jnp.zeros((8, cols), F32)
        brgb[p] = jnp.concatenate(parts + [z], axis=0).astype(BF16)

    def colors_three(i):
        for k in range(3):
            colors(7 + 3 * i + k)

    loop(0, 6, colors_three)

    mean, rstd = norm[0:1], norm[1:2]
    offset = mean * rstd
    sact, lat, wdt = sact.ready(), lat.ready(), wdt.ready()
    dxh = o_dxh.ref

    def last_two(i, carry):
        return last(9 + 2 * i, last(8 + 2 * i, carry))

    def last(p, carry):
        s, q = carry
        y = tn(brgb[pl.ds(p - 1, 3)].reshape(96, cols), wdt[...])
        for i in range(2):
            r = 2 * (p - 8) + i
            d = y[:, i * 128 : (i + 1) * 128] * sact[r].astype(F32)
            xh = lat[r].astype(F32) * rstd - offset
            dxh[r] = d.astype(BF16)
            s = s + jnp.sum(d.reshape(cols // 8, 8, 128), axis=0)
            q = q + jnp.sum((d * xh).reshape(cols // 8, 8, 128), axis=0)
        return s, q

    z = jnp.zeros((8, 128), F32)
    s, q = lax.fori_loop(0, 8, last_two, (z, z))
    o_dxh.send()
    sums[...] = jnp.broadcast_to(group_rows(s, q), sums.shape)


def final_kernel(count, lat, dxh, norm, sums, out_hbm, lbuf, dbuf, obuf, sems):
    rows = obuf.shape[0]
    parts = 4
    size = rows // parts
    arriving, leaving = [], []
    for k in range(parts):
        at = pl.ds(k * size, size)
        arriving.append(pltpu.make_async_copy(lat.at[at], lbuf.at[at], sems.at[k]))
        arriving.append(pltpu.make_async_copy(dxh.at[at], dbuf.at[at], sems.at[parts + k]))
        leaving.append(pltpu.make_async_copy(obuf.at[at], out_hbm.at[at], sems.at[2 * parts + k]))
    for c in arriving:
        c.start()
    mean, rstd = norm[0:1], norm[1:2]
    n1, n2 = group_values(sums[...], count)
    b = rstd * rstd * n2
    c = rstd * n1 - b * mean

    def row(r):
        obuf[r] = (dbuf[r].astype(F32) * rstd - lbuf[r].astype(F32) * b - c).astype(BF16)

    for k in range(parts):
        arriving[2 * k].wait()
        arriving[2 * k + 1].wait()
        loop(k * size // 2, (k + 1) * size // 2, lambda i: (row(2 * i), row(2 * i + 1)))
        leaving[k].start()
    for x in leaving:
        x.wait()


def placed_at(x, space):
    return x if INTERPRET else pltpu.with_memory_space_constraint(x, space)


class Arriving:
    def __init__(self, src, dst, sem, whole):
        self.dst = whole
        self.copy = pltpu.make_async_copy(src, dst, sem)
        self.copy.start()

    def ready(self):
        self.copy.wait()
        return self.dst


class Leaving:
    def __init__(self, src, dst, sem, whole):
        self.ref = whole
        self.copy = pltpu.make_async_copy(src, dst, sem)

    def send(self):
        self.copy.start()


def call(kernel, outs, scratch, args, kinds, out_kinds, order=None, spans=None, out_spans=None):
    spaces = {"s": pltpu.SMEM, "a": pl.ANY,  "d": pl.ANY, "v": pltpu.VMEM, "m": pltpu.VMEM}
    late_in = [i for i, k in enumerate(kinds) if k == "d"]
    late_out = [i for i, k in enumerate(out_kinds) if k == "d"]
    buffers = [pltpu.VMEM(args[i].shape, args[i].dtype) for i in late_in]
    buffers += [pltpu.VMEM(*outs[i]) for i in late_out]
    sems = [pltpu.SemaphoreType.DMA((len(buffers),))] if buffers else []

    def body(*refs):
        refs = list(refs)
        n_in, n_out = len(args), len(outs)
        ins, results, rest = refs[:n_in], refs[n_in : n_in + n_out], refs[n_in + n_out :]
        own, extra = rest[: len(scratch)], rest[len(scratch) :]
        leaving = []
        for i in order or late_in:
            j = late_in.index(i)
            at = (spans or {}).get(i, slice(None))
            ins[i] = Arriving(ins[i].at[at], extra[j].at[at], extra[-1].at[j], extra[j])
        for j, i in enumerate(late_out):
            k = len(late_in) + j
            at = (out_spans or {}).get(i, slice(None))
            results[i] = Leaving(extra[k].at[at], results[i].at[at], extra[-1].at[k], extra[k])
            leaving.append(results[i])
        kernel(*ins, *results, *own)
        for x in leaving:
            x.copy.wait()

    return pl.pallas_call(
        body,
        out_shape=[jax.ShapeDtypeStruct(s, d) if INTERPRET else pltpu.HBM(s, d) for s, d in outs],
        in_specs=[pl.BlockSpec(memory_space=spaces[k]) for k in kinds],
        out_specs=[pl.BlockSpec(memory_space=spaces[k]) for k in out_kinds],
        scratch_shapes=list(scratch) + buffers + sems,
        compiler_params=pltpu.CompilerParams(vmem_limit_bytes=VMEM_LIMIT),
        interpret=INTERPRET,
    )(*[a if k == "s" else placed_at(a, pltpu.VMEM if k == "m" else pltpu.HBM) for a, k in zip(args, kinds)])


def local(
    latent,
    gain,
    bias,
    decoder_weight,
    decoder_bias,
    first_weight,
    first_bias,
    second_weight,
    second_bias,
    third_weight,
    third_bias,
    fourth_weight,
    fourth_bias,
    exemplar_low,
    exemplar_high,
):
    rows, cols, channels = latent.shape
    nrow, ncol = lax.axis_size("row"), lax.axis_size("col")
    n = nrow * ncol
    both = ("row", "col")
    h = HALO
    width = cols + 2 * h
    half = width // 2
    pairs = (rows + 2 * h) // 2
    image_rows, image_cols = rows * nrow, cols * ncol
    count = image_rows * image_cols * (channels // GROUPS)
    dims = (rows, cols, image_rows, image_cols, count)

    def shifted(x, axis, step):
        size = lax.axis_size(axis)
        return lax.ppermute(x, axis, [(i, i + step) for i in range(size) if 0 <= i + step < size])

    def everyone(x):
        return lax.all_to_all(x, both, 0, 0, tiled=True)

    up = shifted(latent[rows - h :], "row", 1)
    down = shifted(latent[:h], "row", -1)
    (mine,) = call(lambda *r: stats_kernel(n, *r), [((n, 128), F32)], [], [latent], "d", "v")
    stats = everyone(mine)
    right_edge, left_edge = call(
        slab_kernel,
        [((2 * pairs, h, 128), BF16)] * 2,
        [],
        [latent, up, down],
        "vvv",
        "vv",
    )
    left = shifted(right_edge, "col", 1)
    right = shifted(left_edge, "col", -1)

    idx = jnp.stack([lax.axis_index("row"), lax.axis_index("col"), jnp.int32(0)]).astype(jnp.int32)
    vecs = jnp.concatenate(
        [
            gain,
            bias,
            first_bias,
            first_bias,
            second_bias,
            second_bias,
            third_bias,
            fourth_bias,
            jnp.zeros((256,), F32),
        ]
    ).reshape(8, 128)
    dec = jnp.pad(jnp.transpose(decoder_weight, (0, 1, 3, 2)), ((0, 0), (0, 0), (0, 1), (0, 0)))
    fst = jnp.pad(first_weight, ((0, 0), (0, 0), (0, 1), (0, 0)))
    sources = [
        dec.reshape(36, 128),
        fst.reshape(36, 64),
        second_weight,
        third_weight,
        fourth_weight,
        *narrow_tables(),
    ]
    shapes = ((72, 256), (96, 128), (256, 384), (256, 768), (512, 768))
    ahead = call(forward_weights, [(x, BF16) for x in shapes], [], sources, "v" * 7, "v" * 5)
    shapes = ((512, 768), (512, 384), (256, 384), (72, 128), (96, 256))
    back = call(backward_weights, [(x, BF16) for x in shapes], [], sources, "v" * 7, "v" * 5)

    states = call(
        lambda *r: forward_kernel(dims, *r),
        [
            ((256, 128), F32),
            ((8, 128), F32),
            ((pairs, width, 128), BF16),
            ((pairs, width, 128), BF16),
            ((pairs, width, 128), BF16),
            ((pairs, half, 128), BF16),
            ((pairs, half, 128), BF16),
            ((pairs, half, 128), BF16),
            ((rows, cols, 128), BF16),
        ],
        [
            pltpu.VMEM((2 * pairs, width, 128), BF16),
            pltpu.VMEM((pairs, 72, 256), F32),
            pltpu.VMEM((pairs, 32, 256), BF16),
            pltpu.VMEM((pairs, width, 128), BF16),
            pltpu.VMEM((pairs, width, 128), BF16),
            pltpu.VMEM((pairs // 2, half, 128), BF16),
            pltpu.VMEM((pairs // 2, half, 128), BF16),
            pltpu.VMEM((half, width), BF16),
            pltpu.VMEM((pairs, half, 128), BF16),
            pltpu.VMEM((pairs, half, 128), BF16),
            pltpu.VMEM((width, 128), BF16),
            pltpu.VMEM((half, 128), BF16),
            pltpu.VMEM((half, 128), BF16),
            pltpu.VMEM((4 * width + 16, 768), F32),
            pltpu.VMEM((4 * width + 16, 768), F32),
            pltpu.SemaphoreType.DMA((5,)),
        ],
        [idx, decoder_bias, latent, up, down, left, right, stats, vecs, *ahead],
        "ssaaammmv" + "d" * 5,
        "vv" + "d" * 7,
        out_spans={
            2: slice(7, 25),
            3: slice(6, 26),
            4: slice(6, 26),
            5: slice(4, 28),
            6: slice(4, 28),
            7: slice(4, 28),
        },
    )
    gram, norm = states[:2]
    mine = everyone(gram).reshape(n, 256 // n, 128).sum(axis=0)
    totals = everyone(jnp.broadcast_to(mine[None], (n, 256 // n, 128)).reshape(256, 128))
    exlow = jnp.tile(exemplar_low, (2, 2))

    dxh, sums, loss = call(
        lambda *r: backward_kernel(dims, *r),
        [((rows, cols, 128), BF16), ((n, 128), F32), ((8, 128), F32)],
        [
            pltpu.VMEM((256, 128), BF16),
            pltpu.VMEM((256, 128), BF16),
            pltpu.VMEM((pairs, half, 128), BF16),
            pltpu.VMEM((pairs, half, 128), BF16),
            pltpu.VMEM((pairs, width, 128), BF16),
            pltpu.VMEM((pairs, width, 128), BF16),
            pltpu.VMEM((width, width), BF16),
            pltpu.VMEM((pairs, 72, 256), F32),
            pltpu.VMEM((pairs, 32, cols), BF16),
            pltpu.VMEM((4 * width + 16, 768), F32),
            pltpu.VMEM((4 * width + 16, 768), F32),
        ],
        [idx, totals, exlow, exemplar_high, *states[2:], latent, norm, *back],
        "smvv" + "d" * 8 + "v" + "d" * 5,
        "dvv",
        order=(8, 9, 13, 7, 14, 5, 6, 15, 4, 16, 10, 11, 17),
        spans={4: slice(7, 25), 5: slice(6, 26), 6: slice(6, 26), 7: slice(4, 28), 8: slice(4, 28), 9: slice(4, 28)},
    )
    sums = everyone(sums)

    tile = (rows, cols, channels)
    (out,) = call(
        lambda *r: final_kernel(count, *r),
        [(tile, BF16)],
        [pltpu.VMEM(tile, BF16)] * 3 + [pltpu.SemaphoreType.DMA((12,))],
        [latent, dxh, norm, sums],
        "aavm",
        "a",
    )
    return out, loss[0, 0]


def solution(mesh):
    placed = (P("row", "col", None),) + (P(),) * 14
    return jax.shard_map(
        local, mesh=mesh, in_specs=placed, out_specs=(P("row", "col", None), P()), check_vma=False
    )
```
